512 devices in a mesh: blk: 32 (over x, z_lo), rep: 16 (over z_hi, y, core).
Axes of the slice: x: 4, y: 4, z: 16 (z_hi: 2, z_lo: 8; z = z_hi * 8 + z_lo), core: 2. Of those that a mesh axis runs over, the one named last changes fastest.
Arguments:
- signals: bfloat16 [32768, 8192], P('rep', 'blk'), may hold values from -6 to 6
- omega: float32 [32, 5, 256, 256], P('blk', None, 'rep'), may hold values from -1.2 to 3, as said below
- pattern: int32 [32, 5], P('blk'), may hold values from 0 to 31, as said below
Outputs:
- omega_next: float32 [32, 5, 256, 256], P('blk', None, 'rep')
The draws below stay inside these ranges and needn't reach their ends.
Inputs may be any that keep to these rules, and one draw needn't show every extreme that they name: pattern[i, 0] = i. For two distinct whole numbers A and B from 1 to 15, the same in every row, pattern[i, 1] to pattern[i, 4] are i + A, i - A, i + B and i - B modulo 32 in some order, the same order in every row. Omega is symmetric: omega[i, k] is the transpose of omega[pattern[i, k], k2] where pattern[pattern[i, k], k2] = i. The diagonal entries of omega[i, 0] lie between 1 and 3.
All inputs are finite; a program needn't handle non-finite values.
Results may differ from the reference program's by a relative error of at most 0.0033.
Values may be sent and summed in bfloat16 or wider, within the bound.
A program may use at most 128 MiB of HBM per device.

```python
import jax
import jax.numpy as jnp
from jax import lax

TILE = 256
K = 5
NB = 32
VOXELS = 8192
TIME = 32768


def pattern_offsets(key):
    inner = jax.random.fold_in(key, 11)
    first_key, second_key, order_key = jax.random.split(inner, 3)
    half = NB // 2
    first = jax.random.randint(first_key, (), 1, half).astype(jnp.int32)
    step_draw = jax.random.randint(second_key, (), 1, half - 1).astype(jnp.int32)
    second = (1 + jnp.mod(first - 1 + step_draw, half - 1)).astype(jnp.int32)
    canon = jnp.stack([jnp.zeros((), jnp.int32), first, NB - first, second, NB - second]).astype(jnp.int32)
    slot_perm = jax.random.permutation(order_key, 4).astype(jnp.int32)
    full_perm = jnp.concatenate([jnp.zeros((1,), jnp.int32), slot_perm + 1]).astype(jnp.int32)
    return (canon, full_perm)


def draw_pattern(key, part):
    canon, full_perm = pattern_offsets(key)
    offsets = canon[full_perm]
    row_ids = jnp.arange(NB, dtype=jnp.int32)
    return jnp.mod(row_ids[:, None] + offsets[None, :], NB).astype(jnp.int32)


def draw_omega(key, part):
    canon, full_perm = pattern_offsets(key)
    raw_key, diag_key = jax.random.split(jax.random.fold_in(key, 23), 2)
    raw_tiles = jax.random.uniform(raw_key, (NB, 3, TILE, TILE), jnp.float32, -0.45, 0.45)
    row_ids = jnp.arange(NB, dtype=jnp.int32)
    identity = jnp.eye(TILE, dtype=jnp.float32)
    diag_values = jax.random.uniform(diag_key, (NB, TILE), jnp.float32, 1.0, 3.0)
    base = raw_tiles[:, 0]
    diagonal_tile = 0.5 * (base + jnp.swapaxes(base, 1, 2))
    diagonal_tile = diagonal_tile * (1.0 - identity) + identity * diag_values[:, :, None]
    pieces = [diagonal_tile]
    for pair_index in range(2):
        offset = canon[1 + 2 * pair_index]
        lower_ids = jnp.mod(row_ids + NB - offset, NB)
        pair_raw = raw_tiles[:, 1 + pair_index]
        upper_tile = pair_raw
        lower_tile = jnp.swapaxes(pair_raw[lower_ids], 1, 2)
        pieces.append(upper_tile)
        pieces.append(lower_tile)
    stacked = jnp.stack(pieces, axis=1)
    return stacked[:, full_perm]


def block_scale(key, shape, shards, low, high):
    level, own = 1.0, jax.random.fold_in(key, 6)
    for position, shards_of in shards:
        steps = jnp.exp(jax.random.uniform(jax.random.fold_in(own, position), (shards_of,), jnp.float32, low / len(shards), high / len(shards)))
        level = level * jnp.repeat(steps, shape[position] // shards_of).reshape([-1 if axis == position else 1 for axis in range(len(shape))])
    return level


def noise(key, extent, spread, reach, cuts=(), kind=jnp.bfloat16):
    drawn = jax.random.normal(key, extent, jnp.float32) * spread
    if len(cuts) > 0:
        drawn = block_scale(key, extent, cuts, -0.22, 0.18) * drawn
    return jnp.clip(drawn, min=-reach, max=reach).astype(kind)


def setup_inputs(seed: int = 0) -> dict:
    key_of = jax.random.split(jax.random.key(seed), 4)
    return {
        "signals": noise(key_of[0], (TIME, VOXELS), 1.0, 6.0, ((0, 16), (1, 32))),
        "omega": draw_omega(jax.random.fold_in(key_of[3], 71), 0),
        "pattern": draw_pattern(jax.random.fold_in(key_of[3], 71), 0),
    }


def reference(signals, omega, pattern):
    time_length = signals.shape[0]
    blocks = signals.reshape(time_length, NB, TILE).transpose(1, 0, 2)
    weights = omega.astype(jnp.bfloat16)

    def make_mixed(block_row):
        total = jnp.zeros((time_length, TILE), jnp.float32)
        for slot_index in range(K):
            partner = blocks[pattern[block_row, slot_index]]
            total = total + jnp.dot(partner, weights[block_row, slot_index].T, preferred_element_type=jnp.float32)
        return total.astype(jnp.bfloat16)

    rows_all = jnp.arange(NB, dtype=jnp.int32)
    mixed = lax.map(make_mixed, rows_all)

    def make_left(block_row):
        return jnp.stack([jnp.dot(mixed[block_row].T, blocks[pattern[block_row, slot_index]], preferred_element_type=jnp.float32) for slot_index in range(K)])

    left_terms = lax.map(make_left, rows_all)
    identity = jnp.eye(TILE, dtype=jnp.float32)

    def make_update(block_row):
        results = []
        for slot_index in range(K):
            column = pattern[block_row, slot_index]
            mirror = jnp.argmax(pattern[column] == block_row).astype(jnp.int32)
            gradient = (left_terms[block_row, slot_index] + left_terms[column, mirror].T) / (2.0 * time_length)
            current = omega[block_row, slot_index]
            if slot_index == 0:
                diag_values = jnp.sum(current * identity, axis=1)
                gradient = gradient - identity * (1.0 / diag_values)[:, None]
            value = current - 0.5 * gradient
            shrunk = jnp.sign(value) * jnp.maximum(jnp.abs(value) - 0.05, 0.0)
            if slot_index == 0:
                shrunk = jnp.where(identity > 0.5, value, shrunk)
            results.append(shrunk)
        return jnp.stack(results)

    return lax.map(make_update, rows_all)
```

```python
import jax
import jax.numpy as jnp
from jax import lax
from jax.sharding import Mesh
from jax.sharding import PartitionSpec as P

STEP_SIZE = 0.5
PENALTY = 0.1
REP = ("zh", "y", "c")


def fine_mesh(mesh):
    return Mesh(mesh.devices.reshape(4, 8, 2, 4, 2), ("x", "zl", "zh", "y", "c"))


def per_device(signals, omega, pattern):
    x_size = lax.axis_size("x")
    zl_size = lax.axis_size("zl")
    team_count = x_size * zl_size
    replica_count = lax.axis_size(REP)
    team_index = lax.axis_index(("x", "zl"))
    replica_index = lax.axis_index(REP)
    slot_count, tile_rows, width = omega.shape[1:]
    time_length = signals.shape[0] * replica_count
    offsets = jnp.mod(pattern[0] - team_index, team_count)

    own = signals.reshape(zl_size, signals.shape[0] // zl_size, width)
    blocks = lax.all_to_all(own, "zl", 0, 0, tiled=True)
    blocks = lax.all_gather(blocks, "x", axis=0, tiled=True)
    panels = lax.all_gather(omega.astype(jnp.bfloat16), REP, axis=2, tiled=True)
    panels = lax.all_gather(panels, "zl", axis=0, tiled=True)

    rows = lax.axis_index("x") * zl_size + jnp.arange(zl_size, dtype=jnp.int32)
    columns = jnp.mod(rows[:, None] + offsets[None, :], team_count)
    gathered = blocks[columns]
    mixed = jnp.einsum("jktc,jkdc->jtd", gathered, panels, preferred_element_type=jnp.float32).astype(jnp.bfloat16)
    left = jnp.einsum("jtd,jktc->jkdc", mixed, gathered, preferred_element_type=jnp.float32)

    own_terms = lax.psum_scatter(left, REP, scatter_dimension=2, tiled=True)
    own_terms = lax.psum_scatter(own_terms, "zl", scatter_dimension=0, tiled=True)[0]
    flipped = lax.all_to_all(own_terms, REP, 2, 1, tiled=True)
    flipped = jnp.swapaxes(flipped, 1, 2)
    match = offsets[None, :] == jnp.mod(team_count - offsets, team_count)[:, None]
    mirror = jnp.argmax(match, axis=1)
    outgoing = flipped[mirror]
    for level in range(team_count.bit_length() - 1):
        step = 1 << level
        route = [((i + step) % team_count, i) for i in range(team_count)]
        shifted = lax.ppermute(outgoing, ("x", "zl"), route)
        chosen = jnp.mod(offsets // step, 2) == 1
        outgoing = jnp.where(chosen[:, None, None], shifted, outgoing)

    gradient = (own_terms + outgoing) / (2.0 * time_length)
    tiles = omega[0]
    column_ids = jnp.arange(width, dtype=jnp.int32)
    row_ids = replica_index * tile_rows + jnp.arange(tile_rows, dtype=jnp.int32)
    diagonal = column_ids[None, :] == row_ids[:, None]
    diagonal = diagonal[None] & (offsets == 0)[:, None, None]
    gradient = gradient - jnp.where(diagonal, 1.0 / jnp.where(diagonal, tiles, 1.0), 0.0)
    value = tiles - STEP_SIZE * gradient
    shrunk = jnp.sign(value) * jnp.maximum(jnp.abs(value) - STEP_SIZE * PENALTY, 0.0)
    return jnp.where(diagonal, value, shrunk)[None]


def solution(mesh):
    return jax.shard_map(
        per_device,
        mesh=fine_mesh(mesh),
        in_specs=(P(REP, ("x", "zl")), P(("x", "zl"), None, REP, None), P(("x", "zl"), None)),
        out_specs=P(("x", "zl"), None, REP, None),
        check_vma=False,
    )
```

```python
import jax
import jax.numpy as jnp
from jax import lax
from jax.experimental import pallas as pl
from jax.experimental.pallas import tpu as pltpu
from jax.sharding import Mesh
from jax.sharding import PartitionSpec as P

STEP_SIZE = 0.5
PENALTY = 0.1
REP = ("zh", "y", "c")
MESH = pl.DeviceIdType.MESH
NX, NZ, NH, NY, NC = 4, 8, 2, 4, 2
Z_ORDER = (4, 5, 6, 7, 1, 2, 3)


def fine_mesh(mesh):
    return Mesh(mesh.devices.reshape(NX, NZ, NH, NY, NC), ("x", "zl", "zh", "y", "c"))


def flip(value, bits):
    for level in range(3):
        weight = 1 << level
        if bits & weight:
            value = value + weight * (1 - 2 * ((value // weight) % 2))
    return value


def remote(src, dst, send, recv, where):
    return pltpu.make_async_remote_copy(
        src_ref=src, dst_ref=dst, send_sem=send, recv_sem=recv, device_id=where, device_id_type=MESH
    )


def exchange_kernel(
    sig, wsh, xout, wout, local_sem, zs, zr, xs_sem, xr, rs, bs, br, ws, wr, ys, yr, cs, cr
):
    x, zl, zh = lax.axis_index("x"), lax.axis_index("zl"), lax.axis_index("zh")
    y, c = lax.axis_index("y"), lax.axis_index("c")
    right, left = {"x": (x + 1) % NX}, {"x": (x + NX - 1) % NX}
    sibling = {"c": 1 - c}
    place = zh * NZ + zl
    ring = NH * NZ
    up, down = (place + 1) % ring, (place + ring - 1) % ring
    up_id = {"zh": up // NZ, "zl": up % NZ}
    down_id = {"zh": down // NZ, "zl": down % NZ}

    barrier = pltpu.get_barrier_semaphore()
    peers = [{"zl": flip(zl, s)} for s in range(1, NZ)] + [right, left, sibling, up_id, down_id]
    peers += [{"y": (y + d) % NY} for d in range(1, NY)]
    for peer in peers:
        pl.semaphore_signal(barrier, inc=1, device_id=peer, device_id_type=MESH)
    pl.semaphore_wait(barrier, len(peers))

    base = c * (NX * NZ)
    mine = base + x * NZ + zl
    own = pltpu.make_async_copy(sig.at[zl], xout.at[mine], local_sem.at[0])
    own.start()
    own_w = pltpu.make_async_copy(wsh, wout.at[c, y, zl, zh], local_sem.at[1])
    own_w.start()
    z_copies = {}
    for s in Z_ORDER:
        peer = flip(zl, s)
        copy = remote(sig.at[peer], xout.at[mine], zs.at[s - 1], zr.at[s - 1], {"zl": peer})
        copy.start()
        z_copies[s] = copy

    def block(dx, s):
        return base + ((x + dx) % NX) * NZ + flip(zl, s)

    def to_sibling(index):
        remote(xout.at[index], xout.at[index], bs, br, sibling).start()

    x_copies = {}

    def spread(s):
        here = xout.at[block(0, s)]
        pair = (
            remote(here, here, xs_sem.at[0, s], xr.at[0, s], right),
            remote(here, here, xs_sem.at[1, s], xr.at[1, s], left),
        )
        for copy in pair:
            copy.start()
        to_sibling(block(0, s))
        x_copies[s] = pair

    relay_copies = {}
    half = xout.shape[1] // 2

    def relay(s):
        pair = []
        for way, (dx, start, where) in enumerate(((NX - 1, 0, right), (1, half, left))):
            x_copies[s][way].wait_recv()
            part = xout.at[block(dx, s), pl.ds(start, half)]
            copy = remote(part, part, rs.at[0, way, s], rs.at[1, way, s], where)
            copy.start()
            to_sibling(block(dx, s))
            pair.append(copy)
        relay_copies[s] = pair

    def finish(s):
        for copy in relay_copies[s]:
            copy.wait_recv()
        to_sibling(block(2, s))

    def shard(origin):
        return wout.at[c, y, origin % NZ, origin // NZ]

    w_copies = []

    def w_step(t):
        if t > 0:
            for copy in w_copies[t - 1]:
                copy.wait_recv()
        pair = []
        if t < 8:
            piece = shard((place + ring - t) % ring)
            pair.append(remote(wsh if t == 0 else piece, piece, ws.at[0, t], wr.at[0, t], up_id))
        if t < 7:
            piece = shard((place + t) % ring)
            pair.append(remote(wsh if t == 0 else piece, piece, ws.at[1, t], wr.at[1, t], down_id))
        for copy in pair:
            copy.start()
        w_copies.append(pair)

    y_copies = []

    def w_spread():
        for copy in w_copies[7]:
            copy.wait_recv()
        for d in range(1, NY):
            copy = remote(wout.at[c, y], wout.at[c, y], ys.at[d - 1], yr.at[d - 1], {"y": (y + d) % NY})
            copy.start()
            y_copies.append(copy)

    c_copies = []

    def w_sibling(d):
        if d > 0:
            y_copies[d - 1].wait_recv()
        part = wout.at[c, (y + NY - d) % NY, pl.ds(4 * (1 - c), 4)]
        copy = remote(part, part, cs.at[d], cr.at[d], sibling)
        copy.start()
        c_copies.append(copy)

    own.wait()
    spread(0)
    own_w.wait()
    for t in range(3):
        w_step(t)
    order = (0,) + Z_ORDER
    for i in range(1, NZ):
        z_copies[order[i]].wait_recv()
        spread(order[i])
        relay(order[i - 1])
        if i >= 2:
            finish(order[i - 2])
        if i == 1:
            w_step(3)
            w_step(4)
        if i == 2:
            w_step(5)
            w_step(6)
        if i == 3:
            w_step(7)
            w_spread()
            w_sibling(0)
    relay(order[NZ - 1])
    finish(order[NZ - 2])
    for d in range(1, NY):
        w_sibling(d)
    finish(order[NZ - 1])

    for copy in z_copies.values():
        copy.wait_send()
    for s in range(NZ):
        for copy in x_copies[s]:
            copy.wait_send()
        for copy in relay_copies[s]:
            copy.wait_send()
    for pair in w_copies:
        for copy in pair:
            copy.wait_send()
    for copy in y_copies:
        copy.wait_send()
    for copy in c_copies:
        copy.wait()
    count = NX * NZ
    whole = remote(xout.at[pl.ds(base, count)], xout.at[pl.ds(count - base, count)], bs, br, sibling)
    whole.wait()


def exchange(signals, shard):
    rows = signals.shape[0] // NZ
    width = signals.shape[1]
    dma = pltpu.SemaphoreType.DMA
    any_spec = pl.BlockSpec(memory_space=pl.ANY)
    return pl.pallas_call(
        exchange_kernel,
        out_shape=(
            jax.ShapeDtypeStruct((NC * NX * NZ, rows, width), signals.dtype),
            jax.ShapeDtypeStruct((NC, NY, NZ, NH) + shard.shape, shard.dtype),
        ),
        in_specs=[any_spec, any_spec],
        out_specs=(any_spec, any_spec),
        scratch_shapes=[
            dma((2,)),
            dma((NZ - 1,)),
            dma((NZ - 1,)),
            dma((2, NZ)),
            dma((2, NZ)),
            dma((2, 2, NZ)),
            dma,
            dma,
            dma((2, 8)),
            dma((2, 8)),
            dma((NY - 1,)),
            dma((NY - 1,)),
            dma((NY,)),
            dma((NY,)),
        ],
        compiler_params=pltpu.CompilerParams(collective_id=0, has_side_effects=True),
        name="exchange",
    )(signals.reshape(NZ, rows, width), shard)


def product_kernel(scalars, x0, x1, x2, x3, x4, w, out):
    blocks = (x0, x1, x2, x3, x4)
    halves = []
    for part in range(NC):
        total = None
        for k, xk in enumerate(blocks):
            panel = jnp.concatenate(
                [
                    w[cc, yy, 0, hh, 16 * k : 16 * k + 16, :]
                    for hh in range(NH)
                    for yy in range(NY)
                    for cc in range(NC)
                ],
                axis=0,
            )
            term = lax.dot_general(panel, xk[part, 0], (((1,), (1,)), ((), ())), preferred_element_type=jnp.float32)
            total = term if total is None else total + term
        halves.append(total.astype(jnp.bfloat16))
    for k, xk in enumerate(blocks):
        left = jnp.dot(halves[0], xk[0, 0], preferred_element_type=jnp.float32)
        left = left + jnp.dot(halves[1], xk[1, 0], preferred_element_type=jnp.float32)
        left = left.astype(jnp.bfloat16)
        for hh in range(NH):
            for yy in range(NY):
                start = hh * 128 + yy * 32
                out[yy, 0, k, hh] = left[start : start + 32, :]


def products(offsets, blocks, panels):
    count = NX * NZ
    x, c = lax.axis_index("x"), lax.axis_index("c")
    rows, width = blocks.shape[1:]
    lines = x * NZ + 4 * c + jnp.arange(4, dtype=jnp.int32)
    columns = jnp.mod(lines[:, None] + offsets[None, :], count).reshape(-1)
    scalars = jnp.concatenate([columns, 4 * c + jnp.arange(4, dtype=jnp.int32)]).astype(jnp.int32)

    def x_spec(k):
        return pl.BlockSpec((NC, 1, rows, width), lambda j, sc, k=k: (0, sc[5 * j + k], 0, 0))

    shape = (NY, 4, 5, NH, 32, width)
    return pl.pallas_call(
        product_kernel,
        out_shape=jax.ShapeDtypeStruct(shape, jnp.bfloat16),
        grid_spec=pltpu.PrefetchScalarGridSpec(
            num_scalar_prefetch=1,
            grid=(4,),
            in_specs=[x_spec(k) for k in range(5)]
            + [pl.BlockSpec((NC, NY, 1, NH, 80, width), lambda j, sc: (0, 0, sc[20 + j], 0, 0, 0))],
            out_specs=pl.BlockSpec((NY, 1, 5, NH, 32, width), lambda j, sc: (0, j, 0, 0, 0, 0)),
        ),
        compiler_params=pltpu.CompilerParams(vmem_limit_bytes=32 << 20),
        name="products",
    )(scalars, *([blocks.reshape(NC, count, rows, width)] * 5), panels)


def sum_kernel(parts, out, own, yrecv, held, zrecv, own_sem, ys, yr, zs, zr, self_sem):
    zl, zh = lax.axis_index("zl"), lax.axis_index("zh")
    y, c = lax.axis_index("y"), lax.axis_index("c")
    place = zh * NZ + zl
    ring = NH * NZ

    barrier = pltpu.get_barrier_semaphore()
    for d in range(1, NY):
        pl.semaphore_signal(barrier, inc=1, device_id={"y": (y + d) % NY}, device_id_type=MESH)
    me = place * NC + c
    for d in range(1, ring * NC):
        other = (me + d) % (ring * NC)
        pl.semaphore_signal(
            barrier,
            inc=1,
            device_id={"zh": other // (NZ * NC), "zl": (other // NC) % NZ, "c": other % NC},
            device_id_type=MESH,
        )
    pl.semaphore_wait(barrier, NY - 1 + ring * NC - 1)

    load = pltpu.make_async_copy(parts.at[y], own, own_sem)
    load.start()
    y_copies = []
    for i in range(4):
        j = (zl + i) % 4
        line = []
        for d in range(1, NY):
            to = (y + d) % NY
            copy = remote(parts.at[to, j], yrecv.at[d - 1, j], ys.at[i, d - 1], yr.at[i, d - 1], {"y": to})
            copy.start()
            line.append(copy)
        y_copies.append(line)
    load.wait()

    def final(j, hh, cc):
        return remote(
            held.at[j, hh, cc],
            zrecv.at[place],
            zs.at[j, hh, cc],
            zr.at[place],
            {"zl": 4 * c + j, "zh": hh, "c": cc},
        )

    def is_me(j, hh, cc):
        return (4 * c + j == zl) & (hh == zh) & (cc == c)

    for i in range(4):
        j = (zl + i) % 4
        for copy in y_copies[i]:
            copy.wait_recv()
        total = own[j].astype(jnp.float32)
        for d in range(NY - 1):
            total = total + yrecv[d, j].astype(jnp.float32)
        total = total.astype(jnp.bfloat16)
        for hh in range(NH):
            for cc in range(NC):
                held[j, hh, cc] = total[:, hh, 16 * cc : 16 * cc + 16, :]

                @pl.when(is_me(j, hh, cc))
                def _(j=j, hh=hh, cc=cc):
                    copy = pltpu.make_async_copy(held.at[j, hh, cc], zrecv.at[place], self_sem)
                    copy.start()
                    copy.wait()

                @pl.when(jnp.logical_not(is_me(j, hh, cc)))
                def _(j=j, hh=hh, cc=cc):
                    final(j, hh, cc).start()

    source_core = zl // 4
    total = None
    for d in range(ring):
        p = (place + d) % ring

        def wait_one(p=p):
            remote(held.at[0, 0, 0], zrecv.at[p], zs.at[0, 0, 0], zr.at[p], {"c": 1 - c}).wait_recv()

        if d == 0:
            pl.when(source_core != c)(wait_one)
        else:
            wait_one()
        term = zrecv[p].astype(jnp.float32)
        total = term if total is None else total + term
    out[...] = total

    for i in range(4):
        j = (zl + i) % 4
        for copy in y_copies[i]:
            copy.wait_send()
        for hh in range(NH):
            for cc in range(NC):

                @pl.when(jnp.logical_not(is_me(j, hh, cc)))
                def _(j=j, hh=hh, cc=cc):
                    final(j, hh, cc).wait_send()


def tile_sums(parts):
    width = parts.shape[-1]
    dma = pltpu.SemaphoreType.DMA
    bf16 = jnp.bfloat16
    return pl.pallas_call(
        sum_kernel,
        out_shape=jax.ShapeDtypeStruct((5, 16, width), jnp.float32),
        in_specs=[pl.BlockSpec(memory_space=pl.ANY)],
        out_specs=pl.BlockSpec(memory_space=pltpu.VMEM),
        scratch_shapes=[
            pltpu.VMEM((4, 5, NH, 32, width), bf16),
            pltpu.VMEM((NY - 1, 4, 5, NH, 32, width), bf16),
            pltpu.VMEM((4, NH, NC, 5, 16, width), bf16),
            pltpu.VMEM((NH * NZ, 5, 16, width), bf16),
            dma,
            dma((4, NY - 1)),
            dma((4, NY - 1)),
            dma((4, NH, NC)),
            dma((NH * NZ,)),
            dma,
        ],
        compiler_params=pltpu.CompilerParams(collective_id=1, has_side_effects=True, vmem_limit_bytes=32 << 20),
        name="tile_sums",
    )(parts)


def per_device(signals, omega, pattern):
    team_count = NX * NZ
    replica_count = lax.axis_size(REP)
    team_index = lax.axis_index(("x", "zl"))
    replica_index = lax.axis_index(REP)
    slot_count, tile_rows, width = omega.shape[1:]
    time_length = signals.shape[0] * replica_count
    offsets = jnp.mod(pattern[0] - team_index, team_count)

    shard = omega[0].astype(jnp.bfloat16).reshape(slot_count * tile_rows, width)
    blocks, panels = exchange(signals, shard)
    own_terms = tile_sums(products(offsets, blocks, panels))

    flipped = lax.all_to_all(own_terms, REP, 2, 1, tiled=True)
    flipped = jnp.swapaxes(flipped, 1, 2)
    match = offsets[None, :] == jnp.mod(team_count - offsets, team_count)[:, None]
    mirror = jnp.argmax(match, axis=1)
    outgoing = flipped[mirror]
    for level in range(team_count.bit_length() - 1):
        step = 1 << level
        route = [((i + step) % team_count, i) for i in range(team_count)]
        shifted = lax.ppermute(outgoing, ("x", "zl"), route)
        chosen = jnp.mod(offsets // step, 2) == 1
        outgoing = jnp.where(chosen[:, None, None], shifted, outgoing)

    gradient = (own_terms + outgoing) / (2.0 * time_length)
    tiles = omega[0]
    column_ids = jnp.arange(width, dtype=jnp.int32)
    row_ids = replica_index * tile_rows + jnp.arange(tile_rows, dtype=jnp.int32)
    diagonal = column_ids[None, :] == row_ids[:, None]
    diagonal = diagonal[None] & (offsets == 0)[:, None, None]
    gradient = gradient - jnp.where(diagonal, 1.0 / jnp.where(diagonal, tiles, 1.0), 0.0)
    value = tiles - STEP_SIZE * gradient
    shrunk = jnp.sign(value) * jnp.maximum(jnp.abs(value) - STEP_SIZE * PENALTY, 0.0)
    return jnp.where(diagonal, value, shrunk)[None]


def solution(mesh):
    return jax.shard_map(
        per_device,
        mesh=fine_mesh(mesh),
        in_specs=(P(REP, ("x", "zl")), P(("x", "zl"), None, REP, None), P(("x", "zl"), None)),
        out_specs=P(("x", "zl"), None, REP, None),
        check_vma=False,
    )
```

```python
import jax
import jax.numpy as jnp
from jax import lax
from jax.experimental import pallas as pl
from jax.experimental.pallas import tpu as pltpu
from jax.sharding import Mesh
from jax.sharding import PartitionSpec as P

STEP_SIZE = 0.5
PENALTY = 0.1
REP = ("zh", "y", "c")
MESH = pl.DeviceIdType.MESH
NX, NZ, NH, NY, NC = 4, 8, 2, 4, 2


def fine_mesh(mesh):
    return Mesh(mesh.devices.reshape(NX, NZ, NH, NY, NC), ("x", "zl", "zh", "y", "c"))


def flip(value, bits):
    for level in range(3):
        weight = 1 << level
        if bits & weight:
            value = value + weight * (1 - 2 * ((value // weight) % 2))
    return value


def remote(src, dst, send, recv, where):
    return pltpu.make_async_remote_copy(
        src_ref=src, dst_ref=dst, send_sem=send, recv_sem=recv, device_id=where, device_id_type=MESH
    )


def exchange_kernel(
    sig, wsh, xout, wout, local_sem, zs, zr, xs_sem, xr, rs, bs, br, ws, wr, ys, yr, qs, qr, cs, cr
):
    x, zl, zh = lax.axis_index("x"), lax.axis_index("zl"), lax.axis_index("zh")
    y, c = lax.axis_index("y"), lax.axis_index("c")
    right, left = {"x": (x + 1) % NX}, {"x": (x + NX - 1) % NX}
    sibling = {"c": 1 - c}
    place = zh * NZ + zl
    ring = NH * NZ
    up, down = (place + 1) % ring, (place + ring - 1) % ring
    up_id = {"zh": up // NZ, "zl": up % NZ}
    down_id = {"zh": down // NZ, "zl": down % NZ}

    barrier = pltpu.get_barrier_semaphore()
    peers = [{"zl": flip(zl, s)} for s in range(1, NZ)] + [right, left, sibling, up_id, down_id]
    peers += [{"y": (y + d) % NY} for d in range(1, NY)]
    for peer in peers:
        pl.semaphore_signal(barrier, inc=1, device_id=peer, device_id_type=MESH)
    pl.semaphore_wait(barrier, len(peers))

    base = c * (NX * NZ)
    mine = base + x * NZ + zl
    own = pltpu.make_async_copy(sig.at[zl], xout.at[mine], local_sem.at[0])
    own.start()
    own_w = pltpu.make_async_copy(wsh, wout.at[c, y, zl, zh], local_sem.at[1])
    own_w.start()
    z_copies = {}

    def z_start(s):
        peer = flip(zl, s)
        copy = remote(sig.at[peer], xout.at[mine], zs.at[s - 1], zr.at[s - 1], {"zl": peer})
        copy.start()
        z_copies[s] = copy

    for s in (4, 1, 2, 3, 5):
        z_start(s)

    def block(dx, s):
        return base + ((x + dx) % NX) * NZ + flip(zl, s)

    def to_sibling(index):
        remote(xout.at[index], xout.at[index], bs, br, sibling).start()

    x_copies = {}

    def spread(s):
        here = xout.at[block(0, s)]
        pair = (
            remote(here, here, xs_sem.at[0, s], xr.at[0, s], right),
            remote(here, here, xs_sem.at[1, s], xr.at[1, s], left),
        )
        for copy in pair:
            copy.start()
        to_sibling(block(0, s))
        x_copies[s] = pair

    relay_copies = {}
    half = xout.shape[1] // 2

    def relay(s):
        pair = []
        for way, (dx, start, where) in enumerate(((NX - 1, 0, right), (1, half, left))):
            x_copies[s][way].wait_recv()
            part = xout.at[block(dx, s), pl.ds(start, half)]
            copy = remote(part, part, rs.at[0, way, s], rs.at[1, way, s], where)
            copy.start()
            to_sibling(block(dx, s))
            pair.append(copy)
        relay_copies[s] = pair

    def finish(s):
        for copy in relay_copies[s]:
            copy.wait_recv()
        to_sibling(block(2, s))

    def origin(e):
        return (place + ring - (e + 1) // 2) % ring if e % 2 else (place + e // 2) % ring

    def shard(e, dy=0):
        o = origin(e)
        return wout.at[c, (y + dy) % NY, o % NZ, o // NZ]

    ring_copies = {}

    def w_ring(t):
        for way, e, steps, where in ((0, max(2 * t - 1, 0), 8, up_id), (1, 2 * t, 7, down_id)):
            if t < steps:
                piece = shard(e)
                copy = remote(wsh if t == 0 else piece, piece, ws.at[way, t], wr.at[way, t], where)
                copy.start()
                ring_copies[way, t] = copy

    forward, backward = {"y": (y + 1) % NY}, {"y": (y + NY - 1) % NY}
    y_copies, y_relays = {}, {}

    def w_forward(e):
        here = shard(e)
        for way, where in enumerate((forward, backward)):
            copy = remote(here, here, ys.at[way, e], yr.at[way, e], where)
            copy.start()
            y_copies[way, e] = copy

    def w_relay(e):
        for way, (dy, start, size, where) in enumerate(((NY - 1, 0, 48, forward), (1, 48, 32, backward))):
            y_copies[way, e].wait_recv()
            part = shard(e, dy).at[pl.ds(start, size)]
            copy = remote(part, part, qs.at[way, e], qr.at[way, e], where)
            copy.start()
            y_relays[way, e] = copy

    def w_pass(t):
        for way in range(2):
            if (way, t) in ring_copies:
                ring_copies[way, t].wait_recv()
        if t < 7:
            w_ring(t + 1)
        for way, e in ((0, 2 * t + 1), (1, 2 * t + 2)):
            if (way, t) in ring_copies:
                w_forward(e)

    def w_relays(t):
        for e in (0,) if t < 0 else (2 * t + 1, 2 * t + 2):
            if (0, e) in y_copies:
                w_relay(e)

    c_copies = []

    def w_sibling(dy):
        part = wout.at[c, (y + dy) % NY, pl.ds(4 * (1 - c), 4)]
        copy = remote(part, part, cs.at[dy], cr.at[dy], sibling)
        copy.start()
        c_copies.append(copy)

    w_ring(0)
    own.wait()
    spread(0)
    own_w.wait()
    w_forward(0)
    for i in range(1, NZ):
        z_copies[i].wait_recv()
        if i + 2 in (6, 7):
            z_start(i + 2)
        spread(i)
        relay(i - 1)
        if i >= 2:
            finish(i - 2)
        w_pass(i - 1)
        w_relays(i - 2)
    relay(NZ - 1)
    w_pass(NZ - 1)
    finish(NZ - 2)
    w_sibling(0)
    w_relays(NZ - 2)
    finish(NZ - 1)
    w_relays(NZ - 1)
    for copy in y_relays.values():
        copy.wait_recv()
    for dy in range(1, NY):
        w_sibling(dy)

    for copy in z_copies.values():
        copy.wait_send()
    for s in range(NZ):
        for copy in x_copies[s]:
            copy.wait_send()
        for copy in relay_copies[s]:
            copy.wait_send()
    for group in (ring_copies, y_copies, y_relays):
        for copy in group.values():
            copy.wait_send()
    for copy in c_copies:
        copy.wait()
    count = NX * NZ
    whole = remote(xout.at[pl.ds(base, count)], xout.at[pl.ds(count - base, count)], bs, br, sibling)
    whole.wait()


def exchange(signals, shard):
    rows = signals.shape[0] // NZ
    width = signals.shape[1]
    dma = pltpu.SemaphoreType.DMA
    any_spec = pl.BlockSpec(memory_space=pl.ANY)
    return pl.pallas_call(
        exchange_kernel,
        out_shape=(
            jax.ShapeDtypeStruct((NC * NX * NZ, rows, width), signals.dtype),
            jax.ShapeDtypeStruct((NC, NY, NZ, NH) + shard.shape, shard.dtype),
        ),
        in_specs=[any_spec, any_spec],
        out_specs=(any_spec, any_spec),
        scratch_shapes=[
            dma((2,)),
            dma((NZ - 1,)),
            dma((NZ - 1,)),
            dma((2, NZ)),
            dma((2, NZ)),
            dma((2, 2, NZ)),
            dma,
            dma,
            dma((2, 8)),
            dma((2, 8)),
            dma((2, 16)),
            dma((2, 16)),
            dma((2, 16)),
            dma((2, 16)),
            dma((NY,)),
            dma((NY,)),
        ],
        compiler_params=pltpu.CompilerParams(collective_id=0, has_side_effects=True),
        name="exchange",
    )(signals.reshape(NZ, rows, width), shard)


def product_kernel(scalars, x0, x1, x2, x3, x4, w, out):
    blocks = (x0, x1, x2, x3, x4)
    halves = []
    for part in range(NC):
        total = None
        for k, xk in enumerate(blocks):
            panel = jnp.concatenate(
                [
                    w[cc, yy, 0, hh, 16 * k : 16 * k + 16, :]
                    for hh in range(NH)
                    for yy in range(NY)
                    for cc in range(NC)
                ],
                axis=0,
            )
            term = lax.dot_general(panel, xk[part, 0], (((1,), (1,)), ((), ())), preferred_element_type=jnp.float32)
            total = term if total is None else total + term
        halves.append(total.astype(jnp.bfloat16))
    for k, xk in enumerate(blocks):
        left = jnp.dot(halves[0], xk[0, 0], preferred_element_type=jnp.float32)
        left = left + jnp.dot(halves[1], xk[1, 0], preferred_element_type=jnp.float32)
        left = left.astype(jnp.bfloat16)
        for hh in range(NH):
            for yy in range(NY):
                start = hh * 128 + yy * 32
                out[yy, 0, k, hh] = left[start : start + 32, :]


def products(offsets, blocks, panels):
    count = NX * NZ
    x, c = lax.axis_index("x"), lax.axis_index("c")
    rows, width = blocks.shape[1:]
    lines = x * NZ + 4 * c + jnp.arange(4, dtype=jnp.int32)
    columns = jnp.mod(lines[:, None] + offsets[None, :], count).reshape(-1)
    scalars = jnp.concatenate([columns, 4 * c + jnp.arange(4, dtype=jnp.int32)]).astype(jnp.int32)

    def x_spec(k):
        return pl.BlockSpec((NC, 1, rows, width), lambda j, sc, k=k: (0, sc[5 * j + k], 0, 0))

    shape = (NY, 4, 5, NH, 32, width)
    return pl.pallas_call(
        product_kernel,
        out_shape=jax.ShapeDtypeStruct(shape, jnp.bfloat16),
        grid_spec=pltpu.PrefetchScalarGridSpec(
            num_scalar_prefetch=1,
            grid=(4,),
            in_specs=[x_spec(k) for k in range(5)]
            + [pl.BlockSpec((NC, NY, 1, NH, 80, width), lambda j, sc: (0, 0, sc[20 + j], 0, 0, 0))],
            out_specs=pl.BlockSpec((NY, 1, 5, NH, 32, width), lambda j, sc: (0, j, 0, 0, 0, 0)),
        ),
        compiler_params=pltpu.CompilerParams(vmem_limit_bytes=60 << 20),
        name="products",
    )(scalars, *([blocks.reshape(NC, count, rows, width)] * 5), panels)


def update_kernel(
    pattern, parts, tiles, out, own, yrecv, held, zrecv, msgs, turned, sent, got,
    own_sem, ys, yr, zs, zr, self_sem, ts, tr, hs, hr
):
    x, zl, zh = lax.axis_index("x"), lax.axis_index("zl"), lax.axis_index("zh")
    y, c = lax.axis_index("y"), lax.axis_index("c")
    place = zh * NZ + zl
    ring = NH * NZ
    team = x * NZ + zl
    teams = NX * NZ
    rep = (zh * NY + y) * NC + c
    reps = NH * NY * NC
    source_core = zl // 4

    def rep_id(r):
        return {"zh": r // (NY * NC), "y": (r // NC) % NY, "c": r % NC}

    def team_id(t):
        return {"x": t // NZ, "zl": t % NZ}

    def greet(where):
        pl.semaphore_signal(barrier, inc=1, device_id=where, device_id_type=MESH)

    barrier = pltpu.get_barrier_semaphore()
    for d in range(1, NY):
        greet({"y": (y + d) % NY})
    for d in range(ring):
        p = (place + d) % ring
        where = {"zh": p // NZ, "zl": p % NZ, "c": source_core}
        if d == 0:
            pl.when(source_core != c)(lambda where=where: greet(where))
        else:
            greet(where)
    for d in range(1, reps):
        greet(rep_id((rep + d) % reps))
    for level in range(4):
        for step in (1 << level, teams - (1 << level)):
            greet(team_id((team + step) % teams))
    greetings = NY - 1 + ring - 1 + reps - 1 + 8
    pl.semaphore_wait(barrier, greetings + jnp.where(source_core != c, 1, 0))

    load = pltpu.make_async_copy(parts.at[y], own, own_sem)
    load.start()
    y_copies = []
    for i in range(4):
        j = (zl + i) % 4
        line = []
        for d in range(1, NY):
            to = (y + d) % NY
            copy = remote(parts.at[to, j], yrecv.at[d - 1, j], ys.at[i, d - 1], yr.at[i, d - 1], {"y": to})
            copy.start()
            line.append(copy)
        y_copies.append(line)
    load.wait()

    def final(j, hh, cc):
        return remote(
            held.at[j, hh, cc],
            zrecv.at[place],
            zs.at[j, hh, cc],
            zr.at[place],
            {"zl": 4 * c + j, "zh": hh, "c": cc},
        )

    def is_me(j, hh, cc):
        return (4 * c + j == zl) & (hh == zh) & (cc == c)

    for i in range(4):
        j = (zl + i) % 4
        for copy in y_copies[i]:
            copy.wait_recv()
        total = own[j].astype(jnp.float32)
        for d in range(NY - 1):
            total = total + yrecv[d, j].astype(jnp.float32)
        total = total.astype(jnp.bfloat16)
        for hh in range(NH):
            for cc in range(NC):
                held[j, hh, cc] = total[:, hh, 16 * cc : 16 * cc + 16, :]

                @pl.when(is_me(j, hh, cc))
                def _(j=j, hh=hh, cc=cc):
                    copy = pltpu.make_async_copy(held.at[j, hh, cc], zrecv.at[place], self_sem)
                    copy.start()
                    copy.wait()

                @pl.when(jnp.logical_not(is_me(j, hh, cc)))
                def _(j=j, hh=hh, cc=cc):
                    final(j, hh, cc).start()

    total = None
    for d in range(ring):
        p = (place + d) % ring

        def wait_one(p=p):
            remote(held.at[0, 0, 0], zrecv.at[p], zs.at[0, 0, 0], zr.at[p], {"c": 1 - c}).wait_recv()

        if d == 0:
            pl.when(source_core != c)(wait_one)
        else:
            wait_one()
        term = zrecv[p].astype(jnp.float32)
        total = term if total is None else total + term

    slots = total.shape[0]
    lane = lax.broadcasted_iota(jnp.int32, (16, 128), 1) // 16
    for r in range(reps):
        message = jnp.zeros((16, 128), jnp.float32)
        for k in range(slots):
            piece = total[k, :, 128 * (r // 8) : 128 * (r // 8) + 128]
            shift = (16 * k - 16 * (r % 8)) % 128
            if shift:
                piece = pltpu.roll(piece, shift, 1)
            message = jnp.where(lane == k, piece, message)
        msgs[r] = message
    turn_copies = []
    for d in range(1, reps):
        r = (rep + d) % reps
        copy = remote(msgs.at[r], turned.at[rep], ts.at[d - 1], tr.at[d - 1], rep_id(r))
        copy.start()
        turn_copies.append(copy)
    turned[rep] = msgs[rep]
    for copy in turn_copies:
        copy.wait_recv()
    flipped = jnp.transpose(turned[...].reshape(16 * reps, 128))
    flipped = [flipped[16 * k : 16 * k + 16] for k in range(slots)]

    offset = [(pattern[0, k] - team + teams) % teams for k in range(slots)]
    low = [offset[k] < teams // 2 for k in range(slots)]
    size = [jnp.where(low[k], offset[k], teams - offset[k]) for k in range(slots)]
    first = [size[k] == size[1] for k in range(slots)]

    def pick(values, is_low, is_first):
        chosen = values[slots - 1]
        for k in range(1, slots - 1):
            chosen = jnp.where((low[k] == is_low) & (first[k] == is_first), values[k], chosen)
        return chosen

    sizes = [size[1], pick(size, True, False)]
    ways = []
    for way in range(2):
        ways.append([pick(flipped, way == 1, u == 0) for u in range(2)])
    hops = []
    for level in range(4):
        step = 1 << level
        pair = []
        for way in range(2):
            for u in range(2):
                sent[level, way, u] = ways[way][u]
            to = (team + (teams - step if way == 0 else step)) % teams
            copy = remote(
                sent.at[level, way], got.at[level, way], hs.at[level, way], hr.at[level, way], team_id(to)
            )
            copy.start()
            pair.append(copy)
        for way in range(2):
            pair[way].wait_recv()
            for u in range(2):
                bit = (sizes[u] // step) % 2 == 1
                ways[way][u] = jnp.where(bit, got[level, way, u], ways[way][u])
        hops.append(pair)

    length = 32768.0
    column = lax.broadcasted_iota(jnp.int32, (16, 256), 1)
    row = lax.broadcasted_iota(jnp.int32, (16, 256), 0) + rep * 16
    diagonal = column == row
    for k in range(slots):
        tile = tiles[0, k]
        if k == 0:
            back = flipped[0]
        else:
            one = jnp.where(first[k], ways[0][0], ways[0][1])
            two = jnp.where(first[k], ways[1][0], ways[1][1])
            back = jnp.where(low[k], one, two)
        gradient = (total[k] + back) / (2.0 * length)
        if k == 0:
            inverse = 1.0 / jnp.where(diagonal, tile, 1.0)
            gradient = gradient - jnp.where(diagonal, inverse, 0.0)
        value = tile - STEP_SIZE * gradient
        limit = STEP_SIZE * PENALTY
        shrunk = jnp.where(value > limit, value - limit, jnp.where(value < -limit, value + limit, 0.0))
        if k == 0:
            shrunk = jnp.where(diagonal, value, shrunk)
        out[0, k] = shrunk

    for i in range(4):
        j = (zl + i) % 4
        for copy in y_copies[i]:
            copy.wait_send()
        for hh in range(NH):
            for cc in range(NC):

                @pl.when(jnp.logical_not(is_me(j, hh, cc)))
                def _(j=j, hh=hh, cc=cc):
                    final(j, hh, cc).wait_send()
    for copy in turn_copies:
        copy.wait_send()
    for pair in hops:
        for copy in pair:
            copy.wait_send()


def update(pattern, parts, tiles):
    width = parts.shape[-1]
    dma = pltpu.SemaphoreType.DMA
    bf16, f32 = jnp.bfloat16, jnp.float32
    reps = NH * NY * NC
    return pl.pallas_call(
        update_kernel,
        out_shape=jax.ShapeDtypeStruct(tiles.shape, f32),
        in_specs=[
            pl.BlockSpec(memory_space=pltpu.SMEM),
            pl.BlockSpec(memory_space=pl.ANY),
            pl.BlockSpec(memory_space=pltpu.VMEM),
        ],
        out_specs=pl.BlockSpec(memory_space=pltpu.VMEM),
        scratch_shapes=[
            pltpu.VMEM((4, 5, NH, 32, width), bf16),
            pltpu.VMEM((NY - 1, 4, 5, NH, 32, width), bf16),
            pltpu.VMEM((4, NH, NC, 5, 16, width), bf16),
            pltpu.VMEM((NH * NZ, 5, 16, width), bf16),
            pltpu.VMEM((reps, 16, 128), f32),
            pltpu.VMEM((reps, 16, 128), f32),
            pltpu.VMEM((4, 2, 2, 16, width), f32),
            pltpu.VMEM((4, 2, 2, 16, width), f32),
            dma,
            dma((4, NY - 1)),
            dma((4, NY - 1)),
            dma((4, NH, NC)),
            dma((NH * NZ,)),
            dma,
            dma((reps - 1,)),
            dma((reps - 1,)),
            dma((4, 2)),
            dma((4, 2)),
        ],
        compiler_params=pltpu.CompilerParams(collective_id=1, has_side_effects=True, vmem_limit_bytes=32 << 20),
        name="update",
    )(pattern, parts, tiles)


def per_device(signals, omega, pattern):
    team_count = NX * NZ
    team_index = lax.axis_index(("x", "zl"))
    slot_count, tile_rows, width = omega.shape[1:]
    offsets = jnp.mod(pattern[0] - team_index, team_count)

    shard = omega[0].astype(jnp.bfloat16).reshape(slot_count * tile_rows, width)
    blocks, panels = exchange(signals, shard)
    return update(pattern, products(offsets, blocks, panels), omega)


def solution(mesh):
    return jax.shard_map(
        per_device,
        mesh=fine_mesh(mesh),
        in_specs=(P(REP, ("x", "zl")), P(("x", "zl"), None, REP, None), P(("x", "zl"), None)),
        out_specs=P(("x", "zl"), None, REP, None),
        check_vma=False,
    )
```

```python
import jax
import jax.numpy as jnp
from jax import lax
from jax.experimental import pallas as pl
from jax.experimental.pallas import tpu as pltpu
from jax.sharding import Mesh
from jax.sharding import PartitionSpec as P

STEP_SIZE = 0.5
PENALTY = 0.1
REP = ("zh", "y", "c")
MESH = pl.DeviceIdType.MESH
NX, NZ, NH, NY, NC = 4, 8, 2, 4, 2


def fine_mesh(mesh):
    return Mesh(mesh.devices.reshape(NX, NZ, NH, NY, NC), ("x", "zl", "zh", "y", "c"))


def flip(value, bits):
    for level in range(3):
        weight = 1 << level
        if bits & weight:
            value = value + weight * (1 - 2 * ((value // weight) % 2))
    return value


def remote(src, dst, send, recv, where):
    return pltpu.make_async_remote_copy(
        src_ref=src, dst_ref=dst, send_sem=send, recv_sem=recv, device_id=where, device_id_type=MESH
    )


def step_kernel(
    pattern, sig, tiles, out, wsh, xout, wout, parts, yfar, ysum, ynear, ylast, held, zrecv, msgs, turned, sent, got,
    local_sem, zs, zr, xs_sem, xr, rs, bs, br, ws, wr, ys, yr, qs, qr, cs, cr,
    ps, pr, gs, gr, self_sem, ts, tr, hs, hr
):
    x, zl, zh = lax.axis_index("x"), lax.axis_index("zl"), lax.axis_index("zh")
    y, c = lax.axis_index("y"), lax.axis_index("c")
    right, left = {"x": (x + 1) % NX}, {"x": (x + NX - 1) % NX}
    sibling = {"c": 1 - c}
    place = zh * NZ + zl
    ring = NH * NZ
    up, down = (place + 1) % ring, (place + ring - 1) % ring
    up_id = {"zh": up // NZ, "zl": up % NZ}
    down_id = {"zh": down // NZ, "zl": down % NZ}

    barrier = pltpu.get_barrier_semaphore()
    team = x * NZ + zl
    teams = NX * NZ
    rep = (zh * NY + y) * NC + c
    reps = NH * NY * NC
    source_core = zl // 4

    def rep_id(r):
        return {"zh": r // (NY * NC), "y": (r // NC) % NY, "c": r % NC}

    def team_id(t):
        return {"x": t // NZ, "zl": t % NZ}

    def greet(where):
        pl.semaphore_signal(barrier, inc=1, device_id=where, device_id_type=MESH)

    peers = [{"zl": flip(zl, s)} for s in range(1, NZ)] + [right, left, sibling, up_id, down_id]
    peers += [{"y": (y + d) % NY} for d in range(1, NY)]
    for d in range(1, ring):
        p = (place + d) % ring
        peers.append({"zh": p // NZ, "zl": p % NZ, "c": source_core})
    peers += [rep_id((rep + d) % reps) for d in range(1, reps)]
    for level in range(4):
        peers += [team_id((team + step) % teams) for step in (1 << level, teams - (1 << level))]
    for peer in peers:
        greet(peer)

    @pl.when(source_core != c)
    def _():
        greet(sibling)

    wsh[...] = tiles[0].reshape(wsh.shape).astype(wsh.dtype)
    pl.semaphore_wait(barrier, len(peers) + jnp.where(source_core != c, 1, 0))

    base = c * (NX * NZ)
    mine = base + x * NZ + zl
    own = pltpu.make_async_copy(sig.at[zl], xout.at[mine], local_sem.at[0])
    own.start()
    own_w = pltpu.make_async_copy(wsh, wout.at[c, y, zl, zh], local_sem.at[1])
    own_w.start()
    z_copies = {}

    def z_start(s):
        peer = flip(zl, s)
        copy = remote(sig.at[peer], xout.at[mine], zs.at[s - 1], zr.at[s - 1], {"zl": peer})
        copy.start()
        z_copies[s] = copy

    for s in (4, 1, 2, 3, 5):
        z_start(s)

    def block(dx, s):
        return base + ((x + dx) % NX) * NZ + flip(zl, s)

    def to_sibling(index):
        remote(xout.at[index], xout.at[index], bs, br, sibling).start()

    x_copies = {}

    def spread(s):
        here = xout.at[block(0, s)]
        pair = (
            remote(here, here, xs_sem.at[0, s], xr.at[0, s], right),
            remote(here, here, xs_sem.at[1, s], xr.at[1, s], left),
        )
        for copy in pair:
            copy.start()
        to_sibling(block(0, s))
        x_copies[s] = pair

    relay_copies = {}
    half = xout.shape[1] // 2

    def relay(s):
        pair = []
        for way, (dx, start, where) in enumerate(((NX - 1, 0, right), (1, half, left))):
            x_copies[s][way].wait_recv()
            part = xout.at[block(dx, s), pl.ds(start, half)]
            copy = remote(part, part, rs.at[0, way, s], rs.at[1, way, s], where)
            copy.start()
            to_sibling(block(dx, s))
            pair.append(copy)
        relay_copies[s] = pair

    def finish(s):
        for copy in relay_copies[s]:
            copy.wait_recv()
        to_sibling(block(2, s))

    def origin(e):
        return (place + ring - (e + 1) // 2) % ring if e % 2 else (place + e // 2) % ring

    def shard(e, dy=0):
        o = origin(e)
        return wout.at[c, (y + dy) % NY, o % NZ, o // NZ]

    ring_copies = {}

    def w_ring(t):
        for way, e, steps, where in ((0, max(2 * t - 1, 0), 8, up_id), (1, 2 * t, 7, down_id)):
            if t < steps:
                piece = shard(e)
                copy = remote(wsh if t == 0 else piece, piece, ws.at[way, t], wr.at[way, t], where)
                copy.start()
                ring_copies[way, t] = copy

    forward, backward = {"y": (y + 1) % NY}, {"y": (y + NY - 1) % NY}
    y_copies, y_relays = {}, {}

    def w_forward(e):
        here = shard(e)
        for way, where in enumerate((forward, backward)):
            copy = remote(here, here, ys.at[way, e], yr.at[way, e], where)
            copy.start()
            y_copies[way, e] = copy

    def w_relay(e):
        for way, (dy, start, size, where) in enumerate(((NY - 1, 0, 48, forward), (1, 48, 32, backward))):
            y_copies[way, e].wait_recv()
            part = shard(e, dy).at[pl.ds(start, size)]
            copy = remote(part, part, qs.at[way, e], qr.at[way, e], where)
            copy.start()
            y_relays[way, e] = copy

    def w_pass(t):
        for way in range(2):
            if (way, t) in ring_copies:
                ring_copies[way, t].wait_recv()
        if t < 7:
            w_ring(t + 1)
        for way, e in ((0, 2 * t + 1), (1, 2 * t + 2)):
            if (way, t) in ring_copies:
                w_forward(e)

    def w_relays(t):
        for e in (0,) if t < 0 else (2 * t + 1, 2 * t + 2):
            if (0, e) in y_copies:
                w_relay(e)

    c_copies = []

    def w_sibling(dy):
        part = wout.at[c, (y + dy) % NY, pl.ds(4 * (1 - c), 4)]
        copy = remote(part, part, cs.at[dy], cr.at[dy], sibling)
        copy.start()
        c_copies.append(copy)

    w_ring(0)
    own.wait()
    spread(0)
    own_w.wait()
    w_forward(0)
    for i in range(1, NZ):
        z_copies[i].wait_recv()
        if i + 2 in (6, 7):
            z_start(i + 2)
        spread(i)
        relay(i - 1)
        if i >= 2:
            finish(i - 2)
        w_pass(i - 1)
        w_relays(i - 2)
    relay(NZ - 1)
    w_pass(NZ - 1)
    finish(NZ - 2)
    w_sibling(0)
    w_relays(NZ - 2)
    finish(NZ - 1)
    w_relays(NZ - 1)
    for copy in y_relays.values():
        copy.wait_recv()
    for dy in range(1, NY):
        w_sibling(dy)

    for copy in z_copies.values():
        copy.wait_send()
    for s in range(NZ):
        for copy in x_copies[s]:
            copy.wait_send()
        for copy in relay_copies[s]:
            copy.wait_send()
    for group in (ring_copies, y_copies, y_relays):
        for copy in group.values():
            copy.wait_send()
    for copy in c_copies:
        copy.wait()
    count = NX * NZ
    whole = remote(xout.at[pl.ds(base, count)], xout.at[pl.ds(count - base, count)], bs, br, sibling)
    whole.wait()

    offset = [(pattern[0, k] - team + teams) % teams for k in range(5)]
    y_next, y_last = (y + 1) % NY, (y + NY - 1) % NY
    y_across = (y + 2) % NY

    def y_sends(i):
        j = (zl + i) % 4
        return (
            remote(parts.at[y_across, j, 0], yfar.at[0, j], ps.at[0, i], pr.at[0, i], forward),
            remote(parts.at[y_across, j, 1], yfar.at[1, j], ps.at[1, i], pr.at[1, i], backward),
            remote(parts.at[y_next, j, 1], ynear.at[0, j], ps.at[2, i], pr.at[2, i], forward),
            remote(parts.at[y_last, j, 0], ynear.at[1, j], ps.at[3, i], pr.at[3, i], backward),
        )

    def y_sums(i):
        j = (zl + i) % 4
        return (
            remote(ysum.at[0, j], ylast.at[0, j], ps.at[4, i], pr.at[4, i], forward),
            remote(ysum.at[1, j], ylast.at[1, j], ps.at[5, i], pr.at[5, i], backward),
        )

    def row_products(i, carry):
        j = (zl + i) % 4
        line = x * NZ + 4 * c + j
        columns = [(line + offset[k]) % teams for k in range(5)]
        halves = []
        for part in range(NC):
            total = None
            for k in range(5):
                panel = jnp.concatenate(
                    [
                        wout[cc, yy, 4 * c + j, hh, 16 * k : 16 * k + 16, :]
                        for hh in range(NH)
                        for yy in range(NY)
                        for cc in range(NC)
                    ],
                    axis=0,
                )
                xk = xout[part * teams + columns[k]]
                term = lax.dot_general(panel, xk, (((1,), (1,)), ((), ())), preferred_element_type=jnp.float32)
                total = term if total is None else total + term
            halves.append(total.astype(jnp.bfloat16))
        for k in range(5):
            product = jnp.dot(halves[0], xout[columns[k]], preferred_element_type=jnp.float32)
            product = product + jnp.dot(halves[1], xout[teams + columns[k]], preferred_element_type=jnp.float32)
            product = product.astype(jnp.bfloat16)
            for hh in range(NH):
                for yy in range(NY):
                    start = hh * 128 + yy * 32
                    parts[yy, j, hh, k] = product[start : start + 32, :]
        for copy in y_sends(i):
            copy.start()
        return carry

    lax.fori_loop(0, 4, row_products, 0)

    def final(j, hh, cc):
        return remote(
            held.at[j, hh, cc],
            zrecv.at[place],
            gs.at[j, hh, cc],
            gr.at[place],
            {"zl": 4 * c + j, "zh": hh, "c": cc},
        )

    def is_me(j, hh, cc):
        return (4 * c + j == zl) & (hh == zh) & (cc == c)

    def y_middle(i):
        j = (zl + i) % 4
        sends = y_sends(i)
        for way, near in enumerate((y_next, y_last)):
            sends[way].wait_recv()
            both = parts[near, j, way].astype(jnp.float32) + yfar[way, j].astype(jnp.float32)
            ysum[way, j] = both.astype(jnp.bfloat16)
            y_sums(i)[way].start()

    def y_end(i):
        j = (zl + i) % 4
        sends, sums = y_sends(i), y_sums(i)
        for hh in range(NH):
            sends[3 - hh].wait_recv()
            sums[hh].wait_recv()
            total = parts[y, j, hh].astype(jnp.float32) + ynear[1 - hh, j].astype(jnp.float32)
            total = (total + ylast[hh, j].astype(jnp.float32)).astype(jnp.bfloat16)
            for cc in range(NC):
                held[j, hh, cc] = total[:, 16 * cc : 16 * cc + 16, :]

                @pl.when(is_me(j, hh, cc))
                def _(hh=hh, cc=cc):
                    copy = pltpu.make_async_copy(held.at[j, hh, cc], zrecv.at[place], self_sem)
                    copy.start()
                    copy.wait()

                @pl.when(jnp.logical_not(is_me(j, hh, cc)))
                def _(hh=hh, cc=cc):
                    final(j, hh, cc).start()

    for i in range(4):
        y_middle(i)
        if i:
            y_end(i - 1)
    y_end(3)

    total = None
    for d in range(ring):
        p = (place + d) % ring

        def wait_one(p=p):
            remote(held.at[0, 0, 0], zrecv.at[p], gs.at[0, 0, 0], gr.at[p], sibling).wait_recv()

        if d == 0:
            pl.when(source_core != c)(wait_one)
        else:
            wait_one()
        term = zrecv[p].astype(jnp.float32)
        total = term if total is None else total + term

    slots = total.shape[0]
    lane = lax.broadcasted_iota(jnp.int32, (16, 128), 1) // 16
    for r in range(reps):
        message = jnp.zeros((16, 128), jnp.float32)
        for k in range(slots):
            piece = total[k, :, 128 * (r // 8) : 128 * (r // 8) + 128]
            shift = (16 * k - 16 * (r % 8)) % 128
            if shift:
                piece = pltpu.roll(piece, shift, 1)
            message = jnp.where(lane == k, piece, message)
        msgs[r] = message.astype(msgs.dtype)
    turn_copies = []
    for d in range(1, reps):
        r = (rep + d) % reps
        copy = remote(msgs.at[r], turned.at[rep], ts.at[d - 1], tr.at[d - 1], rep_id(r))
        copy.start()
        turn_copies.append(copy)
    turned[rep] = msgs[rep]
    for copy in turn_copies:
        copy.wait_recv()
    flipped = jnp.transpose(turned[...].astype(jnp.float32).reshape(16 * reps, 128))
    flipped = [flipped[16 * k : 16 * k + 16] for k in range(slots)]

    low = [offset[k] < teams // 2 for k in range(slots)]
    size = [jnp.where(low[k], offset[k], teams - offset[k]) for k in range(slots)]
    first = [size[k] == size[1] for k in range(slots)]

    def pick(values, is_low, is_first):
        chosen = values[slots - 1]
        for k in range(1, slots - 1):
            chosen = jnp.where((low[k] == is_low) & (first[k] == is_first), values[k], chosen)
        return chosen

    sizes = [size[1], pick(size, True, False)]
    ways = []
    for way in range(2):
        ways.append([pick(flipped, way == 1, u == 0) for u in range(2)])
    hops = []
    for level in range(4):
        step = 1 << level
        pair = []
        for way in range(2):
            for u in range(2):
                sent[level, way, u] = ways[way][u].astype(sent.dtype)
            to = (team + (teams - step if way == 0 else step)) % teams
            copy = remote(
                sent.at[level, way], got.at[level, way], hs.at[level, way], hr.at[level, way], team_id(to)
            )
            copy.start()
            pair.append(copy)
        for way in range(2):
            pair[way].wait_recv()
            for u in range(2):
                bit = (sizes[u] // step) % 2 == 1
                ways[way][u] = jnp.where(bit, got[level, way, u].astype(jnp.float32), ways[way][u])
        hops.append(pair)

    length = 32768.0
    column = lax.broadcasted_iota(jnp.int32, (16, 256), 1)
    row = lax.broadcasted_iota(jnp.int32, (16, 256), 0) + rep * 16
    diagonal = column == row
    for k in range(slots):
        tile = tiles[0, k]
        if k == 0:
            back = flipped[0]
        else:
            one = jnp.where(first[k], ways[0][0], ways[0][1])
            two = jnp.where(first[k], ways[1][0], ways[1][1])
            back = jnp.where(low[k], one, two)
        gradient = (total[k] + back) / (2.0 * length)
        if k == 0:
            inverse = 1.0 / jnp.where(diagonal, tile, 1.0)
            gradient = gradient - jnp.where(diagonal, inverse, 0.0)
        value = tile - STEP_SIZE * gradient
        limit = STEP_SIZE * PENALTY
        shrunk = jnp.where(value > limit, value - limit, jnp.where(value < -limit, value + limit, 0.0))
        if k == 0:
            shrunk = jnp.where(diagonal, value, shrunk)
        out[0, k] = shrunk

    for i in range(4):
        j = (zl + i) % 4
        for copy in y_sends(i) + y_sums(i):
            copy.wait_send()
        for hh in range(NH):
            for cc in range(NC):

                @pl.when(jnp.logical_not(is_me(j, hh, cc)))
                def _(j=j, hh=hh, cc=cc):
                    final(j, hh, cc).wait_send()
    for copy in turn_copies:
        copy.wait_send()
    for pair in hops:
        for copy in pair:
            copy.wait_send()


def per_device(signals, omega, pattern):
    rows = signals.shape[0] // NZ
    slots, tile_rows, width = omega.shape[1:]
    dma = pltpu.SemaphoreType.DMA
    bf16, f32 = jnp.bfloat16, jnp.float32
    reps = NH * NY * NC
    ring = NH * NZ
    piece = (slots, 32, width)
    return pl.pallas_call(
        step_kernel,
        out_shape=jax.ShapeDtypeStruct(omega.shape, f32),
        in_specs=[
            pl.BlockSpec(memory_space=pltpu.SMEM),
            pl.BlockSpec(memory_space=pl.ANY),
            pl.BlockSpec(memory_space=pltpu.VMEM),
        ],
        out_specs=pl.BlockSpec(memory_space=pltpu.VMEM),
        scratch_shapes=[
            pltpu.VMEM((slots * tile_rows, width), bf16),
            pltpu.VMEM((NC * NX * NZ, rows, width), bf16),
            pltpu.VMEM((NC, NY, NZ, NH, slots * tile_rows, width), bf16),
            pltpu.VMEM((NY, 4, NH) + piece, bf16),
            pltpu.VMEM((2, 4) + piece, bf16),
            pltpu.VMEM((2, 4) + piece, bf16),
            pltpu.VMEM((2, 4) + piece, bf16),
            pltpu.VMEM((2, 4) + piece, bf16),
            pltpu.VMEM((4, NH, NC, slots, tile_rows, width), bf16),
            pltpu.VMEM((ring, slots, tile_rows, width), bf16),
            pltpu.VMEM((reps, 16, 128), bf16),
            pltpu.VMEM((reps, 16, 128), bf16),
            pltpu.VMEM((4, 2, 2, tile_rows, width), bf16),
            pltpu.VMEM((4, 2, 2, tile_rows, width), bf16),
            dma((2,)),
            dma((NZ - 1,)),
            dma((NZ - 1,)),
            dma((2, NZ)),
            dma((2, NZ)),
            dma((2, 2, NZ)),
            dma,
            dma,
            dma((2, 8)),
            dma((2, 8)),
            dma((2, 16)),
            dma((2, 16)),
            dma((2, 16)),
            dma((2, 16)),
            dma((NY,)),
            dma((NY,)),
            dma((6, 4)),
            dma((6, 4)),
            dma((4, NH, NC)),
            dma((ring,)),
            dma,
            dma((reps - 1,)),
            dma((reps - 1,)),
            dma((4, 2)),
            dma((4, 2)),
        ],
        compiler_params=pltpu.CompilerParams(collective_id=0, has_side_effects=True, vmem_limit_bytes=48 << 20),
        name="step",
    )(pattern, signals.reshape(NZ, rows, width), omega)


def solution(mesh):
    return jax.shard_map(
        per_device,
        mesh=fine_mesh(mesh),
        in_specs=(P(REP, ("x", "zl")), P(("x", "zl"), None, REP, None), P(("x", "zl"), None)),
        out_specs=P(("x", "zl"), None, REP, None),
        check_vma=False,
    )
```

```python
import jax
import jax.numpy as jnp
from jax import lax
from jax.experimental import pallas as pl
from jax.experimental.pallas import tpu as pltpu
from jax.sharding import Mesh
from jax.sharding import PartitionSpec as P

STEP_SIZE = 0.5
PENALTY = 0.1
REP = ("zh", "y", "c")
MESH = pl.DeviceIdType.MESH
NX, NZ, NH, NY, NC = 4, 8, 2, 4, 2


W_FIRST = 0
W_SLOTS = {1: (0,), 2: (1,), 3: (2,), 4: (3,), 5: (4,), 6: (5,), 7: (6,), 9: (7,)}


def fine_mesh(mesh):
    return Mesh(mesh.devices.reshape(NX, NZ, NH, NY, NC), ("x", "zl", "zh", "y", "c"))


def flip(value, bits):
    for level in range(3):
        weight = 1 << level
        if bits & weight:
            value = value + weight * (1 - 2 * ((value // weight) % 2))
    return value


def remote(src, dst, send, recv, where):
    return pltpu.make_async_remote_copy(
        src_ref=src, dst_ref=dst, send_sem=send, recv_sem=recv, device_id=where, device_id_type=MESH
    )


def step_kernel(
    pattern, sig, tiles, out, wsh, xout, wout, parts, yfar, ysum, ynear, ylast, held, zrecv, msgs, turned, sent, got,
    local_sem, zs, zr, xs_sem, xr, rs, bs, br, ws, wr, ys, yr, cs,
    ps, pr, gs, gr, self_sem, ts, tr, hs, hr
):
    x, zl, zh = lax.axis_index("x"), lax.axis_index("zl"), lax.axis_index("zh")
    y, c = lax.axis_index("y"), lax.axis_index("c")
    right, left = {"x": (x + 1) % NX}, {"x": (x + NX - 1) % NX}
    sibling = {"c": 1 - c}
    place = zh * NZ + zl
    ring = NH * NZ
    up, down = (place + 1) % ring, (place + ring - 1) % ring
    up_id = {"zh": up // NZ, "zl": up % NZ}
    down_id = {"zh": down // NZ, "zl": down % NZ}

    barrier = pltpu.get_barrier_semaphore()
    team = x * NZ + zl
    teams = NX * NZ
    rep = (zh * NY + y) * NC + c
    reps = NH * NY * NC
    source_core = zl // 4

    def rep_id(r):
        return {"zh": r // (NY * NC), "y": (r // NC) % NY, "c": r % NC}

    def team_id(t):
        return {"x": t // NZ, "zl": t % NZ}

    def greet(where):
        pl.semaphore_signal(barrier, inc=1, device_id=where, device_id_type=MESH)

    peers = [{"zl": flip(zl, s)} for s in range(1, NZ)] + [right, left, sibling]
    peers += [{"y": (y + d) % NY, "c": cc} for d in range(1, NY) for cc in range(NC)]
    for peer in peers:
        greet(peer)

    @pl.when(zl == NZ - 1)
    def _():
        greet(up_id)

    @pl.when(zl == 0)
    def _():
        greet(down_id)

    across = jnp.where(zl == NZ - 1, 1, 0) + jnp.where(zl == 0, 1, 0)
    wsh[...] = tiles[0].reshape(wsh.shape).astype(wsh.dtype)
    pl.semaphore_wait(barrier, len(peers) + across)

    base = c * (NX * NZ)
    mine = base + x * NZ + zl
    own = pltpu.make_async_copy(sig.at[zl], xout.at[mine], local_sem.at[0])
    own.start()
    own_w = pltpu.make_async_copy(wsh, wout.at[((c * NY + y) * NZ + zl) * NH + zh], local_sem.at[1])
    own_w.start()
    z_copies = {}

    def z_start(s):
        peer = flip(zl, s)
        copy = remote(sig.at[peer], xout.at[mine], zs.at[s - 1], zr.at[s - 1], {"zl": peer})
        copy.start()
        z_copies[s] = copy

    for s in (4, 1, 2, 3, 5):
        z_start(s)

    def block(dx, s):
        return base + ((x + dx) % NX) * NZ + flip(zl, s)

    def to_sibling(index):
        remote(xout.at[index], xout.at[index], bs, br, sibling).start()

    x_copies = {}

    def spread(s):
        here = xout.at[block(0, s)]
        pair = (
            remote(here, here, xs_sem.at[0, s], xr.at[0, s], right),
            remote(here, here, xs_sem.at[1, s], xr.at[1, s], left),
        )
        for copy in pair:
            copy.start()
        to_sibling(block(0, s))
        x_copies[s] = pair

    relay_copies = {}
    half = xout.shape[1] // 2

    def relay(s):
        pair = []
        for way, (dx, start, where) in enumerate(((NX - 1, 0, right), (1, half, left))):
            x_copies[s][way].wait_recv()
            part = xout.at[block(dx, s), pl.ds(start, half)]
            copy = remote(part, part, rs.at[0, way, s], rs.at[1, way, s], where)
            copy.start()
            to_sibling(block(dx, s))
            pair.append(copy)
        relay_copies[s] = pair

    def finish(s):
        for copy in relay_copies[s]:
            copy.wait_recv()
        to_sibling(block(2, s))

    def origin(e):
        return (place + ring - (e + 1) // 2) % ring if e % 2 else (place + e // 2) % ring

    def shard(o):
        return wout.at[((c * NY + y) * NZ + o % NZ) * NH + o // NZ]

    ring_copies = {}

    def w_ring(t):
        for way, e, steps, where in ((0, max(2 * t - 1, 0), 8, up_id), (1, 2 * t, 7, down_id)):
            if t < steps:
                piece = shard(origin(e))
                copy = remote(wsh if t == 0 else piece, piece, ws.at[way, t], wr.at[way, t], where)
                copy.start()
                ring_copies[way, t] = copy

    forward, backward = {"y": (y + 1) % NY}, {"y": (y + NY - 1) % NY}

    def w_forward(e):
        o = origin(e)
        core = (o % NZ) // 4
        for d in (1, 3, 2):
            remote(shard(o), shard(o), ys, yr, {"y": (y + d) % NY, "c": core}).start()

        @pl.when(core != c)
        def _():
            remote(shard(o), shard(o), cs, yr, sibling).start()

    def w_pass(t):
        for way in range(2):
            if (way, t) in ring_copies:
                ring_copies[way, t].wait_recv()
        if t < 7:
            w_ring(t + 1)
        for way, e in ((0, 2 * t + 1), (1, 2 * t + 2)):
            if (way, t) in ring_copies:
                w_forward(e)

    def w_passes(steps):
        for t in steps:
            w_pass(t)

    own.wait()
    spread(0)
    own_w.wait()
    if W_FIRST == 0:
        w_ring(0)
        w_forward(0)
    for i in range(1, NZ):
        z_copies[i].wait_recv()
        if i + 2 in (6, 7):
            z_start(i + 2)
        spread(i)
        relay(i - 1)
        if i >= 2:
            finish(i - 2)
        if i == W_FIRST:
            w_ring(0)
            w_forward(0)
        w_passes(W_SLOTS.get(i, ()))
    w_passes(W_SLOTS.get(8, ()))
    relay(NZ - 1)
    w_passes(W_SLOTS.get(9, ()))
    finish(NZ - 2)
    w_passes(W_SLOTS.get(10, ()))
    finish(NZ - 1)
    w_passes(W_SLOTS.get(11, ()))
    for copy in z_copies.values():
        copy.wait_send()
    for s in range(NZ):
        for copy in x_copies[s]:
            copy.wait_send()
        for copy in relay_copies[s]:
            copy.wait_send()
    for copy in ring_copies.values():
        copy.wait_send()

    def shards(count):
        return wout.at[pl.ds(0, count)]

    remote(shards(3 * ring), shards(3 * ring), ys, yr, sibling).wait_send()
    remote(shards(ring // 2), shards(ring // 2), cs, yr, sibling).wait_send()
    remote(shards(7 * ring // 2), shards(7 * ring // 2), ys, yr, sibling).wait_recv()
    count = NX * NZ
    whole = remote(xout.at[pl.ds(base, count)], xout.at[pl.ds(count - base, count)], bs, br, sibling)
    whole.wait()

    offset = [(pattern[0, k] - team + teams) % teams for k in range(5)]
    y_next, y_last = (y + 1) % NY, (y + NY - 1) % NY
    y_across = (y + 2) % NY

    def y_sends(i):
        j = (zl + i) % 4
        return (
            remote(parts.at[y_across, j, 0], yfar.at[0, j], ps.at[0, i], pr.at[0, i], forward),
            remote(parts.at[y_across, j, 1], yfar.at[1, j], ps.at[1, i], pr.at[1, i], backward),
            remote(parts.at[y_next, j, 1], ynear.at[0, j], ps.at[2, i], pr.at[2, i], forward),
            remote(parts.at[y_last, j, 0], ynear.at[1, j], ps.at[3, i], pr.at[3, i], backward),
        )

    def y_sums(i):
        j = (zl + i) % 4
        return (
            remote(ysum.at[0, j], ylast.at[0, j], ps.at[4, i], pr.at[4, i], forward),
            remote(ysum.at[1, j], ylast.at[1, j], ps.at[5, i], pr.at[5, i], backward),
        )

    def row_products(i, carry):
        j = (zl + i) % 4
        line = x * NZ + 4 * c + j
        columns = [(line + offset[k]) % teams for k in range(5)]
        halves = []
        for part in range(NC):
            total = None
            for k in range(5):
                panel = jnp.concatenate(
                    [
                        wout[((cc * NY + yy) * NZ + 4 * c + j) * NH + hh, 16 * k : 16 * k + 16, :]
                        for hh in range(NH)
                        for yy in range(NY)
                        for cc in range(NC)
                    ],
                    axis=0,
                )
                xk = xout[part * teams + columns[k]]
                term = lax.dot_general(panel, xk, (((1,), (1,)), ((), ())), preferred_element_type=jnp.float32)
                total = term if total is None else total + term
            halves.append(total.astype(jnp.bfloat16))
        for k in range(5):
            product = jnp.dot(halves[0], xout[columns[k]], preferred_element_type=jnp.float32)
            product = product + jnp.dot(halves[1], xout[teams + columns[k]], preferred_element_type=jnp.float32)
            product = product.astype(jnp.bfloat16)
            for hh in range(NH):
                for yy in range(NY):
                    start = hh * 128 + yy * 32
                    parts[yy, j, hh, k] = product[start : start + 32, :]
        for copy in y_sends(i):
            copy.start()
        return carry

    lax.fori_loop(0, 4, row_products, 0)

    def final(j, hh, cc):
        return remote(
            held.at[j, hh, cc],
            zrecv.at[place],
            gs.at[j, hh, cc],
            gr.at[place],
            {"zl": 4 * c + j, "zh": hh, "c": cc},
        )

    def is_me(j, hh, cc):
        return (4 * c + j == zl) & (hh == zh) & (cc == c)

    def y_middle(i):
        j = (zl + i) % 4
        sends = y_sends(i)
        for way, near in enumerate((y_next, y_last)):
            sends[way].wait_recv()
            both = parts[near, j, way].astype(jnp.float32) + yfar[way, j].astype(jnp.float32)
            ysum[way, j] = both.astype(jnp.bfloat16)
            y_sums(i)[way].start()

    def y_end(i):
        j = (zl + i) % 4
        sends, sums = y_sends(i), y_sums(i)
        for hh in range(NH):
            sends[3 - hh].wait_recv()
            sums[hh].wait_recv()
            total = parts[y, j, hh].astype(jnp.float32) + ynear[1 - hh, j].astype(jnp.float32)
            total = (total + ylast[hh, j].astype(jnp.float32)).astype(jnp.bfloat16)
            for cc in range(NC):
                held[j, hh, cc] = total[:, 16 * cc : 16 * cc + 16, :]

                @pl.when(is_me(j, hh, cc))
                def _(hh=hh, cc=cc):
                    copy = pltpu.make_async_copy(held.at[j, hh, cc], zrecv.at[place], self_sem)
                    copy.start()
                    copy.wait()

                @pl.when(jnp.logical_not(is_me(j, hh, cc)))
                def _(hh=hh, cc=cc):
                    final(j, hh, cc).start()

    for i in range(4):
        y_middle(i)
        if i:
            y_end(i - 1)
    y_end(3)

    total = None
    for d in range(ring):
        p = (place + d) % ring

        def wait_one(p=p):
            remote(held.at[0, 0, 0], zrecv.at[p], gs.at[0, 0, 0], gr.at[p], sibling).wait_recv()

        if d == 0:
            pl.when(source_core != c)(wait_one)
        else:
            wait_one()
        term = zrecv[p].astype(jnp.float32)
        total = term if total is None else total + term

    slots = total.shape[0]
    lane = lax.broadcasted_iota(jnp.int32, (16, 128), 1) // 16
    for r in range(reps):
        message = jnp.zeros((16, 128), jnp.float32)
        for k in range(slots):
            piece = total[k, :, 128 * (r // 8) : 128 * (r // 8) + 128]
            shift = (16 * k - 16 * (r % 8)) % 128
            if shift:
                piece = pltpu.roll(piece, shift, 1)
            message = jnp.where(lane == k, piece, message)
        msgs[r] = message.astype(msgs.dtype)
    turn_copies = []
    for d in range(1, reps):
        r = (rep + d) % reps
        copy = remote(msgs.at[r], turned.at[rep], ts.at[d - 1], tr.at[d - 1], rep_id(r))
        copy.start()
        turn_copies.append(copy)
    turned[rep] = msgs[rep]
    for copy in turn_copies:
        copy.wait_recv()
    flipped = jnp.transpose(turned[...].astype(jnp.float32).reshape(16 * reps, 128))
    flipped = [flipped[16 * k : 16 * k + 16] for k in range(slots)]

    low = [offset[k] < teams // 2 for k in range(slots)]
    size = [jnp.where(low[k], offset[k], teams - offset[k]) for k in range(slots)]
    first = [size[k] == size[1] for k in range(slots)]

    def pick(values, is_low, is_first):
        chosen = values[slots - 1]
        for k in range(1, slots - 1):
            chosen = jnp.where((low[k] == is_low) & (first[k] == is_first), values[k], chosen)
        return chosen

    sizes = [size[1], pick(size, True, False)]
    ways = []
    for way in range(2):
        ways.append([pick(flipped, way == 1, u == 0) for u in range(2)])
    hops = []
    for level in range(4):
        step = 1 << level
        pair = []
        for way in range(2):
            for u in range(2):
                sent[level, way, u] = ways[way][u].astype(sent.dtype)
            to = (team + (teams - step if way == 0 else step)) % teams
            copy = remote(
                sent.at[level, way], got.at[level, way], hs.at[level, way], hr.at[level, way], team_id(to)
            )
            copy.start()
            pair.append(copy)
        for way in range(2):
            pair[way].wait_recv()
            for u in range(2):
                bit = (sizes[u] // step) % 2 == 1
                ways[way][u] = jnp.where(bit, got[level, way, u].astype(jnp.float32), ways[way][u])
        hops.append(pair)

    length = 32768.0
    column = lax.broadcasted_iota(jnp.int32, (16, 256), 1)
    row = lax.broadcasted_iota(jnp.int32, (16, 256), 0) + rep * 16
    diagonal = column == row
    for k in range(slots):
        tile = tiles[0, k]
        if k == 0:
            back = flipped[0]
        else:
            one = jnp.where(first[k], ways[0][0], ways[0][1])
            two = jnp.where(first[k], ways[1][0], ways[1][1])
            back = jnp.where(low[k], one, two)
        gradient = (total[k] + back) / (2.0 * length)
        if k == 0:
            inverse = 1.0 / jnp.where(diagonal, tile, 1.0)
            gradient = gradient - jnp.where(diagonal, inverse, 0.0)
        value = tile - STEP_SIZE * gradient
        limit = STEP_SIZE * PENALTY
        shrunk = jnp.where(value > limit, value - limit, jnp.where(value < -limit, value + limit, 0.0))
        if k == 0:
            shrunk = jnp.where(diagonal, value, shrunk)
        out[0, k] = shrunk

    for i in range(4):
        j = (zl + i) % 4
        for copy in y_sends(i) + y_sums(i):
            copy.wait_send()
        for hh in range(NH):
            for cc in range(NC):

                @pl.when(jnp.logical_not(is_me(j, hh, cc)))
                def _(j=j, hh=hh, cc=cc):
                    final(j, hh, cc).wait_send()
    for copy in turn_copies:
        copy.wait_send()
    for pair in hops:
        for copy in pair:
            copy.wait_send()


def per_device(signals, omega, pattern):
    rows = signals.shape[0] // NZ
    slots, tile_rows, width = omega.shape[1:]
    dma = pltpu.SemaphoreType.DMA
    bf16, f32 = jnp.bfloat16, jnp.float32
    reps = NH * NY * NC
    ring = NH * NZ
    piece = (slots, 32, width)
    return pl.pallas_call(
        step_kernel,
        out_shape=jax.ShapeDtypeStruct(omega.shape, f32),
        in_specs=[
            pl.BlockSpec(memory_space=pltpu.SMEM),
            pl.BlockSpec(memory_space=pl.ANY),
            pl.BlockSpec(memory_space=pltpu.VMEM),
        ],
        out_specs=pl.BlockSpec(memory_space=pltpu.VMEM),
        scratch_shapes=[
            pltpu.VMEM((slots * tile_rows, width), bf16),
            pltpu.VMEM((NC * NX * NZ, rows, width), bf16),
            pltpu.VMEM((NC * NY * NZ * NH, slots * tile_rows, width), bf16),
            pltpu.VMEM((NY, 4, NH) + piece, bf16),
            pltpu.VMEM((2, 4) + piece, bf16),
            pltpu.VMEM((2, 4) + piece, bf16),
            pltpu.VMEM((2, 4) + piece, bf16),
            pltpu.VMEM((2, 4) + piece, bf16),
            pltpu.VMEM((4, NH, NC, slots, tile_rows, width), bf16),
            pltpu.VMEM((ring, slots, tile_rows, width), bf16),
            pltpu.VMEM((reps, 16, 128), bf16),
            pltpu.VMEM((reps, 16, 128), bf16),
            pltpu.VMEM((4, 2, 2, tile_rows, width), bf16),
            pltpu.VMEM((4, 2, 2, tile_rows, width), bf16),
            dma((2,)),
            dma((NZ - 1,)),
            dma((NZ - 1,)),
            dma((2, NZ)),
            dma((2, NZ)),
            dma((2, 2, NZ)),
            dma,
            dma,
            dma((2, 8)),
            dma((2, 8)),
            dma,
            dma,
            dma,
            dma((6, 4)),
            dma((6, 4)),
            dma((4, NH, NC)),
            dma((ring,)),
            dma,
            dma((reps - 1,)),
            dma((reps - 1,)),
            dma((4, 2)),
            dma((4, 2)),
        ],
        compiler_params=pltpu.CompilerParams(collective_id=0, has_side_effects=True, vmem_limit_bytes=48 << 20),
        name="step",
    )(pattern, signals.reshape(NZ, rows, width), omega)


def solution(mesh):
    return jax.shard_map(
        per_device,
        mesh=fine_mesh(mesh),
        in_specs=(P(REP, ("x", "zl")), P(("x", "zl"), None, REP, None), P(("x", "zl"), None)),
        out_specs=P(("x", "zl"), None, REP, None),
        check_vma=False,
    )
```

```python
import jax
import jax.numpy as jnp
from jax import lax
from jax.experimental import pallas as pl
from jax.experimental.pallas import tpu as pltpu
from jax.sharding import Mesh
from jax.sharding import PartitionSpec as P

STEP_SIZE = 0.5
PENALTY = 0.1
REP = ("zh", "y", "c")
MESH = pl.DeviceIdType.MESH
NX, NZ, NH, NY, NC = 4, 8, 2, 4, 2


Y_AHEAD = 1
Y_LAG = 0
W_FIRST = 0
W_SLOTS = {1: (0,), 2: (1,), 3: (2,), 4: (3,), 5: (4,), 6: (5,), 7: (6,), 9: (7,)}


def fine_mesh(mesh):
    return Mesh(mesh.devices.reshape(NX, NZ, NH, NY, NC), ("x", "zl", "zh", "y", "c"))


def flip(value, bits):
    for level in range(3):
        weight = 1 << level
        if bits & weight:
            value = value + weight * (1 - 2 * ((value // weight) % 2))
    return value


def remote(src, dst, send, recv, where):
    return pltpu.make_async_remote_copy(
        src_ref=src, dst_ref=dst, send_sem=send, recv_sem=recv, device_id=where, device_id_type=MESH
    )


def step_kernel(
    pattern, sig, tiles, out, wsh, xout, wout, parts, yfar, ysum, ynear, ylast, held, zrecv, msgs, turned, sent, got,
    local_sem, zs, zr, xs_sem, xr, rs, bs, br, ws, wr, ys, yr, cs,
    ps, pr, gs, gr, self_sem, ts, tr, hs, hr
):
    x, zl, zh = lax.axis_index("x"), lax.axis_index("zl"), lax.axis_index("zh")
    y, c = lax.axis_index("y"), lax.axis_index("c")
    right, left = {"x": (x + 1) % NX}, {"x": (x + NX - 1) % NX}
    sibling = {"c": 1 - c}
    place = zh * NZ + zl
    ring = NH * NZ
    up, down = (place + 1) % ring, (place + ring - 1) % ring
    up_id = {"zh": up // NZ, "zl": up % NZ}
    down_id = {"zh": down // NZ, "zl": down % NZ}

    barrier = pltpu.get_barrier_semaphore()
    team = x * NZ + zl
    teams = NX * NZ
    rep = (zh * NY + y) * NC + c
    reps = NH * NY * NC
    source_core = zl // 4

    def rep_id(r):
        return {"zh": r // (NY * NC), "y": (r // NC) % NY, "c": r % NC}

    def team_id(t):
        return {"x": t // NZ, "zl": t % NZ}

    def greet(where):
        pl.semaphore_signal(barrier, inc=1, device_id=where, device_id_type=MESH)

    peers = [{"zl": flip(zl, s)} for s in range(1, NZ)] + [right, left, sibling]
    peers += [{"y": (y + d) % NY, "c": cc} for d in range(1, NY) for cc in range(NC)]
    for peer in peers:
        greet(peer)

    @pl.when(zl == NZ - 1)
    def _():
        greet(up_id)

    @pl.when(zl == 0)
    def _():
        greet(down_id)

    across = jnp.where(zl == NZ - 1, 1, 0) + jnp.where(zl == 0, 1, 0)
    wsh[...] = tiles[0].reshape(wsh.shape).astype(wsh.dtype)
    pl.semaphore_wait(barrier, len(peers) + across)

    base = c * (NX * NZ)
    mine = base + x * NZ + zl
    own = pltpu.make_async_copy(sig.at[zl], xout.at[mine], local_sem.at[0])
    own.start()
    own_w = pltpu.make_async_copy(wsh, wout.at[((c * NY + y) * NZ + zl) * NH + zh], local_sem.at[1])
    own_w.start()
    z_copies = {}

    def z_start(s):
        peer = flip(zl, s)
        copy = remote(sig.at[peer], xout.at[mine], zs.at[s - 1], zr.at[s - 1], {"zl": peer})
        copy.start()
        z_copies[s] = copy

    for s in (4, 1, 2, 3, 5):
        z_start(s)

    def block(dx, s):
        return base + ((x + dx) % NX) * NZ + flip(zl, s)

    def to_sibling(index):
        remote(xout.at[index], xout.at[index], bs, br, sibling).start()

    x_copies = {}

    def spread(s):
        here = xout.at[block(0, s)]
        pair = (
            remote(here, here, xs_sem.at[0, s], xr.at[0, s], right),
            remote(here, here, xs_sem.at[1, s], xr.at[1, s], left),
        )
        for copy in pair:
            copy.start()
        to_sibling(block(0, s))
        x_copies[s] = pair

    relay_copies = {}
    half = xout.shape[1] // 2

    def relay(s):
        pair = []
        for way, (dx, start, where) in enumerate(((NX - 1, 0, right), (1, half, left))):
            x_copies[s][way].wait_recv()
            part = xout.at[block(dx, s), pl.ds(start, half)]
            copy = remote(part, part, rs.at[0, way, s], rs.at[1, way, s], where)
            copy.start()
            to_sibling(block(dx, s))
            pair.append(copy)
        relay_copies[s] = pair

    def finish(s):
        for copy in relay_copies[s]:
            copy.wait_recv()
        to_sibling(block(2, s))

    def origin(e):
        return (place + ring - (e + 1) // 2) % ring if e % 2 else (place + e // 2) % ring

    def shard(o):
        return wout.at[((c * NY + y) * NZ + o % NZ) * NH + o // NZ]

    ring_copies = {}

    def w_ring(t):
        for way, e, steps, where in ((0, max(2 * t - 1, 0), 8, up_id), (1, 2 * t, 7, down_id)):
            if t < steps:
                piece = shard(origin(e))
                copy = remote(wsh if t == 0 else piece, piece, ws.at[way, t], wr.at[way, t], where)
                copy.start()
                ring_copies[way, t] = copy

    forward, backward = {"y": (y + 1) % NY}, {"y": (y + NY - 1) % NY}

    def w_forward(e):
        o = origin(e)
        core = (o % NZ) // 4
        for d in (1, 3, 2):
            remote(shard(o), shard(o), ys, yr, {"y": (y + d) % NY, "c": core}).start()

        @pl.when(core != c)
        def _():
            remote(shard(o), shard(o), cs, yr, sibling).start()

    def w_pass(t):
        for way in range(2):
            if (way, t) in ring_copies:
                ring_copies[way, t].wait_recv()
        if t < 7:
            w_ring(t + 1)
        for way, e in ((0, 2 * t + 1), (1, 2 * t + 2)):
            if (way, t) in ring_copies:
                w_forward(e)

    def w_passes(steps):
        for t in steps:
            w_pass(t)

    own.wait()
    spread(0)
    own_w.wait()
    if W_FIRST == 0:
        w_ring(0)
        w_forward(0)
    for i in range(1, NZ):
        z_copies[i].wait_recv()
        if i + 2 in (6, 7):
            z_start(i + 2)
        spread(i)
        relay(i - 1)
        if i >= 2:
            finish(i - 2)
        if i == W_FIRST:
            w_ring(0)
            w_forward(0)
        w_passes(W_SLOTS.get(i, ()))
    w_passes(W_SLOTS.get(8, ()))
    relay(NZ - 1)
    w_passes(W_SLOTS.get(9, ()))
    finish(NZ - 2)
    w_passes(W_SLOTS.get(10, ()))
    finish(NZ - 1)
    w_passes(W_SLOTS.get(11, ()))
    for copy in z_copies.values():
        copy.wait_send()
    for s in range(NZ):
        for copy in x_copies[s]:
            copy.wait_send()
        for copy in relay_copies[s]:
            copy.wait_send()
    for copy in ring_copies.values():
        copy.wait_send()

    def shards(count):
        return wout.at[pl.ds(0, count)]

    remote(shards(3 * ring), shards(3 * ring), ys, yr, sibling).wait_send()
    remote(shards(ring // 2), shards(ring // 2), cs, yr, sibling).wait_send()
    remote(shards(7 * ring // 2), shards(7 * ring // 2), ys, yr, sibling).wait_recv()
    count = NX * NZ
    whole = remote(xout.at[pl.ds(base, count)], xout.at[pl.ds(count - base, count)], bs, br, sibling)
    whole.wait()

    offset = [(pattern[0, k] - team + teams) % teams for k in range(5)]
    y_next, y_last = (y + 1) % NY, (y + NY - 1) % NY
    y_across = (y + 2) % NY

    def y_sends(i):
        j = (zl + i) % 4
        return (
            remote(parts.at[y_across, j, 0], yfar.at[0, j], ps.at[0, i], pr.at[0, i], forward),
            remote(parts.at[y_across, j, 1], yfar.at[1, j], ps.at[1, i], pr.at[1, i], backward),
            remote(parts.at[y_next, j, 1], ynear.at[0, j], ps.at[2, i], pr.at[2, i], forward),
            remote(parts.at[y_last, j, 0], ynear.at[1, j], ps.at[3, i], pr.at[3, i], backward),
        )

    def y_sums(i):
        j = (zl + i) % 4
        return (
            remote(ysum.at[0, j], ylast.at[0, j], ps.at[4, i], pr.at[4, i], forward),
            remote(ysum.at[1, j], ylast.at[1, j], ps.at[5, i], pr.at[5, i], backward),
        )

    def row_products(i, carry):
        j = (zl + i) % 4
        line = x * NZ + 4 * c + j
        columns = [(line + offset[k]) % teams for k in range(5)]
        halves = []
        for part in range(NC):
            total = None
            for k in range(5):
                panel = jnp.concatenate(
                    [
                        wout[((cc * NY + yy) * NZ + 4 * c + j) * NH + hh, 16 * k : 16 * k + 16, :]
                        for hh in range(NH)
                        for yy in range(NY)
                        for cc in range(NC)
                    ],
                    axis=0,
                )
                xk = xout[part * teams + columns[k]]
                term = lax.dot_general(panel, xk, (((1,), (1,)), ((), ())), preferred_element_type=jnp.float32)
                total = term if total is None else total + term
            halves.append(total.astype(jnp.bfloat16))
        for k in range(5):
            product = jnp.dot(halves[0], xout[columns[k]], preferred_element_type=jnp.float32)
            product = product + jnp.dot(halves[1], xout[teams + columns[k]], preferred_element_type=jnp.float32)
            product = product.astype(jnp.bfloat16)
            for hh in range(NH):
                for yy in range(NY):
                    start = hh * 128 + yy * 32
                    parts[yy, j, hh, k] = product[start : start + 32, :]

        @pl.when(i < Y_AHEAD)
        def _():
            for copy in y_sends(i):
                copy.start()

        return carry

    lax.fori_loop(0, 4, row_products, 0)

    def final(j, hh, cc):
        return remote(
            held.at[j, hh, cc],
            zrecv.at[place],
            gs.at[j, hh, cc],
            gr.at[place],
            {"zl": 4 * c + j, "zh": hh, "c": cc},
        )

    def is_me(j, hh, cc):
        return (4 * c + j == zl) & (hh == zh) & (cc == c)

    def y_middle(i):
        j = (zl + i) % 4
        sends = y_sends(i)
        for way, near in enumerate((y_next, y_last)):
            sends[way].wait_recv()
            both = parts[near, j, way].astype(jnp.float32) + yfar[way, j].astype(jnp.float32)
            ysum[way, j] = both.astype(jnp.bfloat16)
            y_sums(i)[way].start()
        if i + Y_AHEAD < 4:
            for copy in y_sends(i + Y_AHEAD):
                copy.start()

    def y_end(i):
        j = (zl + i) % 4
        sends, sums = y_sends(i), y_sums(i)
        for hh in range(NH):
            sends[3 - hh].wait_recv()
            sums[hh].wait_recv()
            total = parts[y, j, hh].astype(jnp.float32) + ynear[1 - hh, j].astype(jnp.float32)
            total = (total + ylast[hh, j].astype(jnp.float32)).astype(jnp.bfloat16)
            for cc in range(NC):
                held[j, hh, cc] = total[:, 16 * cc : 16 * cc + 16, :]

                @pl.when(is_me(j, hh, cc))
                def _(hh=hh, cc=cc):
                    copy = pltpu.make_async_copy(held.at[j, hh, cc], zrecv.at[place], self_sem)
                    copy.start()
                    copy.wait()

                @pl.when(jnp.logical_not(is_me(j, hh, cc)))
                def _(hh=hh, cc=cc):
                    final(j, hh, cc).start()

    for i in range(4):
        y_middle(i)
        if i >= Y_LAG:
            y_end(i - Y_LAG)
    for i in range(4 - Y_LAG, 4):
        y_end(i)

    total = None
    for d in range(ring):
        p = (place + d) % ring

        def wait_one(p=p):
            remote(held.at[0, 0, 0], zrecv.at[p], gs.at[0, 0, 0], gr.at[p], sibling).wait_recv()

        if d == 0:
            pl.when(source_core != c)(wait_one)
        else:
            wait_one()
        term = zrecv[p].astype(jnp.float32)
        total = term if total is None else total + term

    slots = total.shape[0]
    lane = lax.broadcasted_iota(jnp.int32, (16, 128), 1) // 16
    for r in range(reps):
        message = jnp.zeros((16, 128), jnp.float32)
        for k in range(slots):
            piece = total[k, :, 128 * (r // 8) : 128 * (r // 8) + 128]
            shift = (16 * k - 16 * (r % 8)) % 128
            if shift:
                piece = pltpu.roll(piece, shift, 1)
            message = jnp.where(lane == k, piece, message)
        msgs[r] = message.astype(msgs.dtype)
    turn_copies = []
    for d in range(1, reps):
        r = (rep + d) % reps
        copy = remote(msgs.at[r], turned.at[rep], ts.at[d - 1], tr.at[d - 1], rep_id(r))
        copy.start()
        turn_copies.append(copy)
    turned[rep] = msgs[rep]
    for copy in turn_copies:
        copy.wait_recv()
    flipped = jnp.transpose(turned[...].astype(jnp.float32).reshape(16 * reps, 128))
    flipped = [flipped[16 * k : 16 * k + 16] for k in range(slots)]

    low = [offset[k] < teams // 2 for k in range(slots)]
    size = [jnp.where(low[k], offset[k], teams - offset[k]) for k in range(slots)]
    first = [size[k] == size[1] for k in range(slots)]

    def pick(values, is_low, is_first):
        chosen = values[slots - 1]
        for k in range(1, slots - 1):
            chosen = jnp.where((low[k] == is_low) & (first[k] == is_first), values[k], chosen)
        return chosen

    sizes = [size[1], pick(size, True, False)]
    ways = []
    for way in range(2):
        ways.append([pick(flipped, way == 1, u == 0) for u in range(2)])
    hops = []
    for level in range(4):
        step = 1 << level
        pair = []
        for way in range(2):
            for u in range(2):
                sent[level, way, u] = ways[way][u].astype(sent.dtype)
            to = (team + (teams - step if way == 0 else step)) % teams
            copy = remote(
                sent.at[level, way], got.at[level, way], hs.at[level, way], hr.at[level, way], team_id(to)
            )
            copy.start()
            pair.append(copy)
        for way in range(2):
            pair[way].wait_recv()
            for u in range(2):
                bit = (sizes[u] // step) % 2 == 1
                ways[way][u] = jnp.where(bit, got[level, way, u].astype(jnp.float32), ways[way][u])
        hops.append(pair)

    length = 32768.0
    column = lax.broadcasted_iota(jnp.int32, (16, 256), 1)
    row = lax.broadcasted_iota(jnp.int32, (16, 256), 0) + rep * 16
    diagonal = column == row
    for k in range(slots):
        tile = tiles[0, k]
        if k == 0:
            back = flipped[0]
        else:
            one = jnp.where(first[k], ways[0][0], ways[0][1])
            two = jnp.where(first[k], ways[1][0], ways[1][1])
            back = jnp.where(low[k], one, two)
        gradient = (total[k] + back) / (2.0 * length)
        if k == 0:
            inverse = 1.0 / jnp.where(diagonal, tile, 1.0)
            gradient = gradient - jnp.where(diagonal, inverse, 0.0)
        value = tile - STEP_SIZE * gradient
        limit = STEP_SIZE * PENALTY
        shrunk = jnp.where(value > limit, value - limit, jnp.where(value < -limit, value + limit, 0.0))
        if k == 0:
            shrunk = jnp.where(diagonal, value, shrunk)
        out[0, k] = shrunk

    for i in range(4):
        j = (zl + i) % 4
        for copy in y_sends(i) + y_sums(i):
            copy.wait_send()
        for hh in range(NH):
            for cc in range(NC):

                @pl.when(jnp.logical_not(is_me(j, hh, cc)))
                def _(j=j, hh=hh, cc=cc):
                    final(j, hh, cc).wait_send()
    for copy in turn_copies:
        copy.wait_send()
    for pair in hops:
        for copy in pair:
            copy.wait_send()


def per_device(signals, omega, pattern):
    rows = signals.shape[0] // NZ
    slots, tile_rows, width = omega.shape[1:]
    dma = pltpu.SemaphoreType.DMA
    bf16, f32 = jnp.bfloat16, jnp.float32
    reps = NH * NY * NC
    ring = NH * NZ
    piece = (slots, 32, width)
    return pl.pallas_call(
        step_kernel,
        out_shape=jax.ShapeDtypeStruct(omega.shape, f32),
        in_specs=[
            pl.BlockSpec(memory_space=pltpu.SMEM),
            pl.BlockSpec(memory_space=pl.ANY),
            pl.BlockSpec(memory_space=pltpu.VMEM),
        ],
        out_specs=pl.BlockSpec(memory_space=pltpu.VMEM),
        scratch_shapes=[
            pltpu.VMEM((slots * tile_rows, width), bf16),
            pltpu.VMEM((NC * NX * NZ, rows, width), bf16),
            pltpu.VMEM((NC * NY * NZ * NH, slots * tile_rows, width), bf16),
            pltpu.VMEM((NY, 4, NH) + piece, bf16),
            pltpu.VMEM((2, 4) + piece, bf16),
            pltpu.VMEM((2, 4) + piece, bf16),
            pltpu.VMEM((2, 4) + piece, bf16),
            pltpu.VMEM((2, 4) + piece, bf16),
            pltpu.VMEM((4, NH, NC, slots, tile_rows, width), bf16),
            pltpu.VMEM((ring, slots, tile_rows, width), bf16),
            pltpu.VMEM((reps, 16, 128), bf16),
            pltpu.VMEM((reps, 16, 128), bf16),
            pltpu.VMEM((4, 2, 2, tile_rows, width), bf16),
            pltpu.VMEM((4, 2, 2, tile_rows, width), bf16),
            dma((2,)),
            dma((NZ - 1,)),
            dma((NZ - 1,)),
            dma((2, NZ)),
            dma((2, NZ)),
            dma((2, 2, NZ)),
            dma,
            dma,
            dma((2, 8)),
            dma((2, 8)),
            dma,
            dma,
            dma,
            dma((6, 4)),
            dma((6, 4)),
            dma((4, NH, NC)),
            dma((ring,)),
            dma,
            dma((reps - 1,)),
            dma((reps - 1,)),
            dma((4, 2)),
            dma((4, 2)),
        ],
        compiler_params=pltpu.CompilerParams(collective_id=0, has_side_effects=True, vmem_limit_bytes=48 << 20),
        name="step",
    )(pattern, signals.reshape(NZ, rows, width), omega)


def solution(mesh):
    return jax.shard_map(
        per_device,
        mesh=fine_mesh(mesh),
        in_specs=(P(REP, ("x", "zl")), P(("x", "zl"), None, REP, None), P(("x", "zl"), None)),
        out_specs=P(("x", "zl"), None, REP, None),
        check_vma=False,
    )
```

```python
import jax
import jax.numpy as jnp
from jax import lax
from jax.experimental import pallas as pl
from jax.experimental.pallas import tpu as pltpu
from jax.sharding import Mesh
from jax.sharding import PartitionSpec as P

STEP_SIZE = 0.5
PENALTY = 0.1
REP = ("zh", "y", "c")
MESH = pl.DeviceIdType.MESH
NX, NZ, NH, NY, NC = 4, 8, 2, 4, 2


Y_AHEAD = 1
Y_LAG = 0
W_FIRST = 0
W_SLOTS = {1: (0,), 2: (1,), 3: (2,), 4: (3,), 5: (4,), 6: (5,), 7: (6,), 9: (7,)}


def fine_mesh(mesh):
    return Mesh(mesh.devices.reshape(NX, NZ, NH, NY, NC), ("x", "zl", "zh", "y", "c"))


def flip(value, bits):
    for level in range(3):
        weight = 1 << level
        if bits & weight:
            value = value + weight * (1 - 2 * ((value // weight) % 2))
    return value


def remote(src, dst, send, recv, where):
    return pltpu.make_async_remote_copy(
        src_ref=src, dst_ref=dst, send_sem=send, recv_sem=recv, device_id=where, device_id_type=MESH
    )


def step_kernel(
    pattern, sig, tiles, out, wsh, xout, wout, parts, yfar, ysum, ynear, ylast, held, zrecv, msgs, turned, sent, got,
    local_sem, zs, zr, xs_sem, xr, rs, bs, br, ws, wr, ys, yr, cs,
    ps, pr, gs, gr, self_sem, ts, tr, hs, hr
):
    x, zl, zh = lax.axis_index("x"), lax.axis_index("zl"), lax.axis_index("zh")
    y, c = lax.axis_index("y"), lax.axis_index("c")
    right, left = {"x": (x + 1) % NX}, {"x": (x + NX - 1) % NX}
    sibling = {"c": 1 - c}
    place = zh * NZ + zl
    ring = NH * NZ
    up, down = (place + 1) % ring, (place + ring - 1) % ring
    up_id = {"zh": up // NZ, "zl": up % NZ}
    down_id = {"zh": down // NZ, "zl": down % NZ}

    barrier = pltpu.get_barrier_semaphore()
    team = x * NZ + zl
    teams = NX * NZ
    rep = (zh * NY + y) * NC + c
    reps = NH * NY * NC
    source_core = zl // 4

    def rep_id(r):
        return {"zh": r // (NY * NC), "y": (r // NC) % NY, "c": r % NC}

    def team_id(t):
        return {"x": t // NZ, "zl": t % NZ}

    def greet(where):
        pl.semaphore_signal(barrier, inc=1, device_id=where, device_id_type=MESH)

    peers = [{"zl": flip(zl, s)} for s in range(1, NZ)] + [right, left, sibling]
    peers += [{"y": (y + d) % NY, "c": cc} for d in range(1, NY) for cc in range(NC)]
    for peer in peers:
        greet(peer)

    @pl.when(zl == NZ - 1)
    def _():
        greet(up_id)

    @pl.when(zl == 0)
    def _():
        greet(down_id)

    across = jnp.where(zl == NZ - 1, 1, 0) + jnp.where(zl == 0, 1, 0)
    wsh[...] = tiles[0].reshape(wsh.shape).astype(wsh.dtype)
    pl.semaphore_wait(barrier, len(peers) + across)

    base = c * (NX * NZ)
    mine = base + x * NZ + zl
    own = pltpu.make_async_copy(sig.at[zl], xout.at[mine], local_sem.at[0])
    own.start()
    own_w = pltpu.make_async_copy(wsh, wout.at[((c * NY + y) * NZ + zl) * NH + zh], local_sem.at[1])
    own_w.start()
    z_copies = {}

    def z_start(s):
        peer = flip(zl, s)
        copy = remote(sig.at[peer], xout.at[mine], zs.at[s - 1], zr.at[s - 1], {"zl": peer})
        copy.start()
        z_copies[s] = copy

    for s in (4, 1, 2, 3, 5):
        z_start(s)

    def block(dx, s):
        return base + ((x + dx) % NX) * NZ + flip(zl, s)

    def to_sibling(index):
        remote(xout.at[index], xout.at[index], bs, br, sibling).start()

    x_copies = {}

    def spread(s):
        here = xout.at[block(0, s)]
        pair = (
            remote(here, here, xs_sem.at[0, s], xr.at[0, s], right),
            remote(here, here, xs_sem.at[1, s], xr.at[1, s], left),
        )
        for copy in pair:
            copy.start()
        to_sibling(block(0, s))
        x_copies[s] = pair

    relay_copies = {}
    half = xout.shape[1] // 2

    def relay(s):
        pair = []
        for way, (dx, start, where) in enumerate(((NX - 1, 0, right), (1, half, left))):
            x_copies[s][way].wait_recv()
            part = xout.at[block(dx, s), pl.ds(start, half)]
            copy = remote(part, part, rs.at[0, way, s], rs.at[1, way, s], where)
            copy.start()
            to_sibling(block(dx, s))
            pair.append(copy)
        relay_copies[s] = pair

    def finish(s):
        for copy in relay_copies[s]:
            copy.wait_recv()
        to_sibling(block(2, s))

    def origin(e):
        return (place + ring - (e + 1) // 2) % ring if e % 2 else (place + e // 2) % ring

    def shard(o):
        return wout.at[((c * NY + y) * NZ + o % NZ) * NH + o // NZ]

    ring_copies = {}

    def w_ring(t):
        for way, e, steps, where in ((0, max(2 * t - 1, 0), 8, up_id), (1, 2 * t, 7, down_id)):
            if t < steps:
                piece = shard(origin(e))
                copy = remote(wsh if t == 0 else piece, piece, ws.at[way, t], wr.at[way, t], where)
                copy.start()
                ring_copies[way, t] = copy

    forward, backward = {"y": (y + 1) % NY}, {"y": (y + NY - 1) % NY}

    def w_forward(e):
        o = origin(e)
        core = (o % NZ) // 4
        for d in (1, 3, 2):
            remote(shard(o), shard(o), ys, yr, {"y": (y + d) % NY, "c": core}).start()

        @pl.when(core != c)
        def _():
            remote(shard(o), shard(o), cs, yr, sibling).start()

    def w_pass(t):
        for way in range(2):
            if (way, t) in ring_copies:
                ring_copies[way, t].wait_recv()
        if t < 7:
            w_ring(t + 1)
        for way, e in ((0, 2 * t + 1), (1, 2 * t + 2)):
            if (way, t) in ring_copies:
                w_forward(e)

    def w_passes(steps):
        for t in steps:
            w_pass(t)

    own.wait()
    spread(0)
    own_w.wait()
    if W_FIRST == 0:
        w_ring(0)
        w_forward(0)
    for i in range(1, NZ):
        z_copies[i].wait_recv()
        if i + 2 in (6, 7):
            z_start(i + 2)
        spread(i)
        relay(i - 1)
        if i >= 2:
            finish(i - 2)
        if i == W_FIRST:
            w_ring(0)
            w_forward(0)
        w_passes(W_SLOTS.get(i, ()))
    w_passes(W_SLOTS.get(8, ()))
    relay(NZ - 1)
    w_passes(W_SLOTS.get(9, ()))
    finish(NZ - 2)
    w_passes(W_SLOTS.get(10, ()))
    finish(NZ - 1)
    w_passes(W_SLOTS.get(11, ()))
    for copy in z_copies.values():
        copy.wait_send()
    for s in range(NZ):
        for copy in x_copies[s]:
            copy.wait_send()
        for copy in relay_copies[s]:
            copy.wait_send()
    for copy in ring_copies.values():
        copy.wait_send()

    def shards(count):
        return wout.at[pl.ds(0, count)]

    remote(shards(3 * ring), shards(3 * ring), ys, yr, sibling).wait_send()
    remote(shards(ring // 2), shards(ring // 2), cs, yr, sibling).wait_send()
    remote(shards(7 * ring // 2), shards(7 * ring // 2), ys, yr, sibling).wait_recv()
    count = NX * NZ
    whole = remote(xout.at[pl.ds(base, count)], xout.at[pl.ds(count - base, count)], bs, br, sibling)
    whole.wait()

    offset = [(pattern[0, k] - team + teams) % teams for k in range(5)]
    y_next, y_last = (y + 1) % NY, (y + NY - 1) % NY
    y_across = (y + 2) % NY

    def y_sends(i):
        j = (zl + i) % 4
        return (
            remote(parts.at[y_across, j, 0], yfar.at[0, j], ps.at[0, i], pr.at[0, i], forward),
            remote(parts.at[y_across, j, 1], yfar.at[1, j], ps.at[1, i], pr.at[1, i], backward),
            remote(parts.at[y_next, j, 1], ynear.at[0, j], ps.at[2, i], pr.at[2, i], forward),
            remote(parts.at[y_last, j, 0], ynear.at[1, j], ps.at[3, i], pr.at[3, i], backward),
        )

    def y_sums(i):
        j = (zl + i) % 4
        return (
            remote(ysum.at[0, j], ylast.at[0, j], ps.at[4, i], pr.at[4, i], forward),
            remote(ysum.at[1, j], ylast.at[1, j], ps.at[5, i], pr.at[5, i], backward),
        )

    def row_products(i, carry):
        j = (zl + i) % 4
        line = x * NZ + 4 * c + j
        columns = [(line + offset[k]) % teams for k in range(5)]
        halves = []
        for part in range(NC):
            total = None
            for k in range(5):
                panel = jnp.concatenate(
                    [
                        wout[((cc * NY + yy) * NZ + 4 * c + j) * NH + hh, 16 * k : 16 * k + 16, :]
                        for hh in range(NH)
                        for yy in range(NY)
                        for cc in range(NC)
                    ],
                    axis=0,
                )
                xk = xout[part * teams + columns[k]]
                term = lax.dot_general(panel, xk, (((1,), (1,)), ((), ())), preferred_element_type=jnp.float32)
                total = term if total is None else total + term
            halves.append(total.astype(jnp.bfloat16))
        for k in range(5):
            product = jnp.dot(halves[0], xout[columns[k]], preferred_element_type=jnp.float32)
            product = product + jnp.dot(halves[1], xout[teams + columns[k]], preferred_element_type=jnp.float32)
            product = product.astype(jnp.bfloat16)
            for hh in range(NH):
                for yy in range(NY):
                    start = hh * 128 + yy * 32
                    parts[yy, j, hh, k] = product[start : start + 32, :]

        @pl.when(i < Y_AHEAD)
        def _():
            for copy in y_sends(i):
                copy.start()

        return carry

    lax.fori_loop(0, 4, row_products, 0)

    def final(j, hh, cc):
        return remote(
            held.at[j, hh, cc],
            zrecv.at[place],
            gs.at[j, hh, cc],
            gr.at[place],
            {"zl": 4 * c + j, "zh": hh, "c": cc},
        )

    def is_me(j, hh, cc):
        return (4 * c + j == zl) & (hh == zh) & (cc == c)

    def y_middle(i):
        j = (zl + i) % 4
        sends = y_sends(i)
        for way, near in enumerate((y_next, y_last)):
            sends[way].wait_recv()
            both = parts[near, j, way].astype(jnp.float32) + yfar[way, j].astype(jnp.float32)
            ysum[way, j] = both.astype(jnp.bfloat16)
            y_sums(i)[way].start()
        if i + Y_AHEAD < 4:
            for copy in y_sends(i + Y_AHEAD):
                copy.start()

    def y_end(i):
        j = (zl + i) % 4
        sends, sums = y_sends(i), y_sums(i)
        for hh in range(NH):
            sends[3 - hh].wait_recv()
            sums[hh].wait_recv()
            total = parts[y, j, hh].astype(jnp.float32) + ynear[1 - hh, j].astype(jnp.float32)
            total = (total + ylast[hh, j].astype(jnp.float32)).astype(jnp.bfloat16)
            for cc in range(NC):
                held[j, hh, cc] = total[:, 16 * cc : 16 * cc + 16, :]

                @pl.when(is_me(j, hh, cc))
                def _(hh=hh, cc=cc):
                    copy = pltpu.make_async_copy(held.at[j, hh, cc], zrecv.at[place], self_sem)
                    copy.start()
                    copy.wait()

                @pl.when(jnp.logical_not(is_me(j, hh, cc)))
                def _(hh=hh, cc=cc):
                    final(j, hh, cc).start()

    for i in range(4):
        y_middle(i)
        if i >= Y_LAG:
            y_end(i - Y_LAG)
    for i in range(4 - Y_LAG, 4):
        y_end(i)

    total = None
    for d in range(ring):
        p = (place + d) % ring

        def wait_one(p=p):
            remote(held.at[0, 0, 0], zrecv.at[p], gs.at[0, 0, 0], gr.at[p], sibling).wait_recv()

        if d == 0:
            pl.when(source_core != c)(wait_one)
        else:
            wait_one()
        term = zrecv[p].astype(jnp.float32)
        total = term if total is None else total + term

    slots = total.shape[0]
    lane = lax.broadcasted_iota(jnp.int32, (16, 128), 1) // 16
    for r in range(reps):
        message = jnp.zeros((16, 128), jnp.float32)
        for k in range(slots):
            piece = total[k, :, 128 * (r // 8) : 128 * (r // 8) + 128]
            shift = (16 * k - 16 * (r % 8)) % 128
            if shift:
                piece = pltpu.roll(piece, shift, 1)
            message = jnp.where(lane == k, piece, message)
        msgs[r] = message.astype(msgs.dtype)
    turn_copies = []
    for d in (8, 9, 7, 10, 6, 11, 5, 12, 4, 13, 3, 14, 2, 15, 1):
        r = (rep + d) % reps
        copy = remote(msgs.at[r], turned.at[rep], ts.at[d - 1], tr.at[d - 1], rep_id(r))
        copy.start()
        turn_copies.append(copy)
    turned[rep] = msgs[rep]
    for copy in turn_copies:
        copy.wait_recv()
    flipped = jnp.transpose(turned[...].astype(jnp.float32).reshape(16 * reps, 128))
    flipped = [flipped[16 * k : 16 * k + 16] for k in range(slots)]

    low = [offset[k] < teams // 2 for k in range(slots)]
    size = [jnp.where(low[k], offset[k], teams - offset[k]) for k in range(slots)]
    first = [size[k] == size[1] for k in range(slots)]

    def pick(values, is_low, is_first):
        chosen = values[slots - 1]
        for k in range(1, slots - 1):
            chosen = jnp.where((low[k] == is_low) & (first[k] == is_first), values[k], chosen)
        return chosen

    sizes = [size[1], pick(size, True, False)]
    ways = []
    for way in range(2):
        ways.append([pick(flipped, way == 1, u == 0) for u in range(2)])
    hops = []
    for level in range(5):
        step = 1 << level
        pair = []
        for way in range(2):
            if level:
                hops[level - 1][way].wait_recv()
                for u in range(2):
                    bit = (sizes[u] // (step // 2)) % 2 == 1
                    arrived = got[level - 1, way, u].astype(jnp.float32)
                    ways[way][u] = jnp.where(bit, arrived, ways[way][u])
            if level < 4:
                for u in range(2):
                    sent[level, way, u] = ways[way][u].astype(sent.dtype)
                to = (team + (teams - step if way == 0 else step)) % teams
                copy = remote(
                    sent.at[level, way], got.at[level, way], hs.at[level, way], hr.at[level, way], team_id(to)
                )
                copy.start()
                pair.append(copy)
        hops.append(pair)

    length = 32768.0
    column = lax.broadcasted_iota(jnp.int32, (16, 256), 1)
    row = lax.broadcasted_iota(jnp.int32, (16, 256), 0) + rep * 16
    diagonal = column == row
    for k in range(slots):
        tile = tiles[0, k]
        if k == 0:
            back = flipped[0]
        else:
            one = jnp.where(first[k], ways[0][0], ways[0][1])
            two = jnp.where(first[k], ways[1][0], ways[1][1])
            back = jnp.where(low[k], one, two)
        gradient = (total[k] + back) / (2.0 * length)
        if k == 0:
            inverse = 1.0 / jnp.where(diagonal, tile, 1.0)
            gradient = gradient - jnp.where(diagonal, inverse, 0.0)
        value = tile - STEP_SIZE * gradient
        limit = STEP_SIZE * PENALTY
        shrunk = jnp.where(value > limit, value - limit, jnp.where(value < -limit, value + limit, 0.0))
        if k == 0:
            shrunk = jnp.where(diagonal, value, shrunk)
        out[0, k] = shrunk

    for i in range(4):
        j = (zl + i) % 4
        for copy in y_sends(i) + y_sums(i):
            copy.wait_send()
        for hh in range(NH):
            for cc in range(NC):

                @pl.when(jnp.logical_not(is_me(j, hh, cc)))
                def _(j=j, hh=hh, cc=cc):
                    final(j, hh, cc).wait_send()
    for copy in turn_copies:
        copy.wait_send()
    for pair in hops:
        for copy in pair:
            copy.wait_send()


def per_device(signals, omega, pattern):
    rows = signals.shape[0] // NZ
    slots, tile_rows, width = omega.shape[1:]
    dma = pltpu.SemaphoreType.DMA
    bf16, f32 = jnp.bfloat16, jnp.float32
    reps = NH * NY * NC
    ring = NH * NZ
    piece = (slots, 32, width)
    return pl.pallas_call(
        step_kernel,
        out_shape=jax.ShapeDtypeStruct(omega.shape, f32),
        in_specs=[
            pl.BlockSpec(memory_space=pltpu.SMEM),
            pl.BlockSpec(memory_space=pl.ANY),
            pl.BlockSpec(memory_space=pltpu.VMEM),
        ],
        out_specs=pl.BlockSpec(memory_space=pltpu.VMEM),
        scratch_shapes=[
            pltpu.VMEM((slots * tile_rows, width), bf16),
            pltpu.VMEM((NC * NX * NZ, rows, width), bf16),
            pltpu.VMEM((NC * NY * NZ * NH, slots * tile_rows, width), bf16),
            pltpu.VMEM((NY, 4, NH) + piece, bf16),
            pltpu.VMEM((2, 4) + piece, bf16),
            pltpu.VMEM((2, 4) + piece, bf16),
            pltpu.VMEM((2, 4) + piece, bf16),
            pltpu.VMEM((2, 4) + piece, bf16),
            pltpu.VMEM((4, NH, NC, slots, tile_rows, width), bf16),
            pltpu.VMEM((ring, slots, tile_rows, width), bf16),
            pltpu.VMEM((reps, 16, 128), bf16),
            pltpu.VMEM((reps, 16, 128), bf16),
            pltpu.VMEM((4, 2, 2, tile_rows, width), bf16),
            pltpu.VMEM((4, 2, 2, tile_rows, width), bf16),
            dma((2,)),
            dma((NZ - 1,)),
            dma((NZ - 1,)),
            dma((2, NZ)),
            dma((2, NZ)),
            dma((2, 2, NZ)),
            dma,
            dma,
            dma((2, 8)),
            dma((2, 8)),
            dma,
            dma,
            dma,
            dma((6, 4)),
            dma((6, 4)),
            dma((4, NH, NC)),
            dma((ring,)),
            dma,
            dma((reps - 1,)),
            dma((reps - 1,)),
            dma((4, 2)),
            dma((4, 2)),
        ],
        compiler_params=pltpu.CompilerParams(collective_id=0, has_side_effects=True, vmem_limit_bytes=48 << 20),
        name="step",
    )(pattern, signals.reshape(NZ, rows, width), omega)


def solution(mesh):
    return jax.shard_map(
        per_device,
        mesh=fine_mesh(mesh),
        in_specs=(P(REP, ("x", "zl")), P(("x", "zl"), None, REP, None), P(("x", "zl"), None)),
        out_specs=P(("x", "zl"), None, REP, None),
        check_vma=False,
    )
```
